32 devices in a mesh: groups: 2 (over x), seq: 16 (over z, y, core).
Axes of the slice: x: 2, y: 2, z: 4, core: 2. Of those that a mesh axis runs over, the one named last changes fastest.
Arguments:
- query_seq: bfloat16 [8192, 6144], P(('groups', 'seq')), parts along dimension 0, may hold values from -15 to 15
- key_seq: bfloat16 [8192, 6144], P(('groups', 'seq')), parts along dimension 0, may hold values from -15 to 15
- value_seq: bfloat16 [8192, 6144], P(('groups', 'seq')), parts along dimension 0, may hold values from -288 to 288
- conv_kernel: bfloat16 [3, 4, 6144], replicated, may hold values from -3 to 3
- feature_map: bfloat16 [128, 128], replicated, may hold values from -1.5 to 1.5
- norm_gain: float32 [6144], replicated, may hold values from 0.25 to 1.75
Outputs:
- attended: bfloat16 [8192, 6144], P(('groups', 'seq')), parts along dimension 0
The draws below stay inside these ranges and needn't reach their ends.
There are 2 independent parts, one for each index of `groups`. The reference program is written for one: setup_inputs(seed, part) draws one part's arguments, and reference() takes and returns one part's arrays. A program takes and returns all parts, laid end to end along the dimension named above; an argument that names none is the same for every part. Nothing has to cross between parts.
All inputs are finite; a program needn't handle non-finite values.
Results may differ from the reference program's by a relative error of at most 0.012.
The reference program's roundings to bfloat16 on the way count: a program that leaves them out, or rounds other values in their place, can miss the bound.
Values may be sent and summed in bfloat16 or wider, within the bound.
A program may use at most 128 MiB of HBM per device.

```python
import math
import jax
import jax.numpy as jnp
from jax import lax

H = 48
DH = 128
D = 6144
SPAN = 256
KCONV = 4
TOKENS = 4096


def draw_value_seq(key, part):
    key_noise = jax.random.fold_in(key, 11)
    key_column = jax.random.fold_in(key, 12)
    key_row = jax.random.fold_in(key, 14)
    noise = jnp.clip(jax.random.normal(key_noise, (TOKENS, D), jnp.float32), -4.0, 4.0)
    column = jnp.exp(jax.random.uniform(key_column, (1, D), jnp.float32) * math.log(10.0))
    row_scale = jnp.exp(jax.random.uniform(key_row, (TOKENS, 1), jnp.float32) * math.log(4.0))
    base = noise * column * row_scale
    earlier = jnp.concatenate([jnp.zeros((1, D), jnp.float32), base[:-1]], axis=0)
    return (base - 0.8 * earlier).astype(jnp.bfloat16)


def draw_feature_map(key, part):
    key_sign = jax.random.fold_in(key, 21)
    key_off = jax.random.fold_in(key, 22)
    signs = (jax.random.randint(key_sign, (DH,), 0, 2) * 2 - 1).astype(jnp.float32)
    off_diag = jnp.clip(jax.random.normal(key_off, (DH, DH), jnp.float32), -4.0, 4.0) * (0.45 / math.sqrt(DH - 1))
    eye = jnp.eye(DH, dtype=jnp.float32)
    return (eye * (1.5 * signs)[None, :] + (1.0 - eye) * off_diag).astype(jnp.bfloat16)


def steps_of(own_key, shape, split, least, high):
    def one(position, blocks):
        draws = jax.random.uniform(jax.random.fold_in(jax.random.fold_in(own_key, 6), position), (blocks,), jnp.float32, least / len(split), high / len(split))
        return jnp.repeat(jnp.exp(draws), shape[position] // blocks).reshape((-1,) + (1,) * (len(shape) - position - 1))

    gain = one(*split[0])
    for cut in split[1:]:
        gain = gain * one(*cut)
    return gain


def gaussian(own_key, dims, width, most, cuts=(), kind=jnp.bfloat16):
    entries = width * jax.random.normal(own_key, dims, jnp.float32)
    if cuts:
        entries = entries * steps_of(own_key, dims, cuts, -0.22, 0.18)
    return jnp.clip(entries, -most, most).astype(kind)


def setup_inputs(seed: int = 0, part: int = 0) -> dict:
    splits = jax.random.split(jax.random.key(seed), 7)
    own_keys = jax.random.split(jax.random.fold_in(splits[6], part), 7)
    query_seq = gaussian(own_keys[0], (TOKENS, D), 3.0, 15.0, ((0, 16),))
    key_seq = gaussian(own_keys[1], (TOKENS, D), 3.0, 15.0, ((0, 16),))
    value_seq = draw_value_seq(jax.random.fold_in(jax.random.fold_in(splits[6], part), 71), part)
    conv_kernel = gaussian(splits[3], (3, KCONV, D), KCONV ** -0.5, 3.0)
    feature_map = draw_feature_map(jax.random.fold_in(splits[6], 71), part)
    norm_gain = jnp.clip(1.0 + 0.15 * jax.random.normal(splits[5], (D,), jnp.float32), 0.25, 1.75)
    return {"query_seq": query_seq, "key_seq": key_seq, "value_seq": value_seq, "conv_kernel": conv_kernel, "feature_map": feature_map, "norm_gain": norm_gain}


def short_conv(seq_rows, kernel):
    tap_count = kernel.shape[0]
    length = seq_rows.shape[0]
    padded = jnp.concatenate([jnp.zeros((tap_count - 1, seq_rows.shape[1]), seq_rows.dtype), seq_rows], axis=0)
    summed = jnp.zeros(seq_rows.shape, jnp.float32)
    for offset in range(tap_count):
        window = padded[tap_count - 1 - offset:tap_count - 1 - offset + length]
        summed = summed + kernel[offset].astype(jnp.float32) * window.astype(jnp.float32)
    return summed.astype(jnp.bfloat16)

def feature_rows(conv_rows, feature_map):
    head_rows = conv_rows.reshape(conv_rows.shape[0], H, DH).astype(jnp.float32)
    projected = jnp.einsum('thd,de->the', head_rows, feature_map.astype(jnp.float32))
    return (jax.nn.elu(projected) + 1.0).astype(jnp.bfloat16)

def reference(query_seq, key_seq, value_seq, conv_kernel, feature_map, norm_gain):
    query_conv = short_conv(query_seq, conv_kernel[0])
    key_conv = short_conv(key_seq, conv_kernel[1])
    value_conv = short_conv(value_seq, conv_kernel[2])
    block_count = TOKENS // SPAN
    query_feat = feature_rows(query_conv, feature_map).reshape(block_count, SPAN, H, DH)
    key_feat = feature_rows(key_conv, feature_map).reshape(block_count, SPAN, H, DH)
    value_heads = value_conv.reshape(block_count, SPAN, H, DH)
    causal = jnp.arange(SPAN)[:, None] >= jnp.arange(SPAN)[None, :]

    def advance(prefix, blocks):
        query_blk, key_blk, value_blk = blocks
        query_wide = query_blk.astype(jnp.float32)
        key_wide = key_blk.astype(jnp.float32)
        value_wide = value_blk.astype(jnp.float32)
        scores = jnp.einsum('ihd,jhd->hij', query_wide, key_wide)
        weights = lax.optimization_barrier(jnp.where(causal[None], scores, 0.0).astype(jnp.bfloat16))
        mixed_rows = jnp.einsum('hij,jhd->ihd', weights.astype(jnp.float32), value_wide)
        prefix_bf = lax.optimization_barrier(prefix.astype(jnp.bfloat16))
        mixed_rows = mixed_rows + jnp.einsum('ihd,hde->ihe', query_wide, prefix_bf.astype(jnp.float32))
        kv_state = jnp.einsum('jhd,jhe->hde', key_wide, value_wide)
        return (prefix + kv_state, mixed_rows)
    start_state = jnp.zeros((H, DH, DH), jnp.float32)
    _, mixed_all = lax.scan(advance, start_state, (query_feat, key_feat, value_heads))
    mixed_all = mixed_all.reshape(TOKENS, H, DH)
    inverse_rms = lax.rsqrt(lax.optimization_barrier(jnp.mean(mixed_all * mixed_all, axis=-1, keepdims=True)) + 1e-06)
    normed = (mixed_all * inverse_rms).reshape(TOKENS, D) * norm_gain
    return normed.astype(jnp.bfloat16)
```

```python
import functools

import jax
import jax.numpy as jnp
from jax import lax
from jax.experimental import pallas as pl
from jax.experimental.pallas import tpu as pltpu
from jax.sharding import PartitionSpec as P

MESH = pl.DeviceIdType.MESH
F32 = jnp.float32
BF16 = jnp.bfloat16
RIM = 8
HALO = 4
LANES = 128
X_LAG = 2
Y_LAG = 4
Z_LAG = 4
R_LAG = 4
P_LAG = 2
MIX_LAG = 12


def short_conv(buf, halo, taps, which, col, width, wide):
    tap_count = taps.shape[1]
    length = buf.shape[0]
    out = []
    for j in range(width // LANES):
        lanes = pl.ds(pl.multiple_of(col + j * LANES, LANES), LANES)
        tall = wide.at[j]
        tap_rows = taps[which, :, lanes].astype(F32)
        tall[RIM - HALO : RIM] = halo[which, :, lanes].astype(F32)
        rows = buf[:, lanes].astype(F32)
        tall[RIM:] = rows
        total = tap_rows[0:1] * rows
        for offset in range(1, tap_count):
            total = total + tap_rows[offset : offset + 1] * tall[RIM - offset : RIM - offset + length]
        out.append(total.astype(BF16))
    return jnp.concatenate(out, axis=1)


def features(conv_rows, wide_map):
    projected = jnp.dot(conv_rows, wide_map[...], preferred_element_type=F32)
    return jnp.where(projected > 0, projected + 1.0, jnp.exp(projected)).astype(BF16)


def kernel(
    devices,
    q_hbm,
    k_hbm,
    v_hbm,
    taps,
    feature_map,
    gain,
    out_buf,
    q_buf,
    k_buf,
    v_buf,
    tail,
    halo_out,
    halo,
    wide,
    wide_map,
    q_feat,
    k_feat,
    v_conv,
    mixed,
    own_state,
    x_out,
    x_in,
    raw_out,
    raw_in,
    z_out,
    z_in,
    res_out,
    res_in,
    p_out,
    prefix,
    load_sem,
    tail_sem,
    send_sem,
    halo_sem,
    x_sem,
    raw_sem,
    z_sem,
    res_sem,
    p_sem,
):
    tokens, width = q_buf.shape
    half = tokens // 2
    dim = feature_map.shape[0]
    pair = 2 * dim
    chunk = 2 * pair
    chunks = width // chunk
    pieces = halo_sem.shape[1]
    per_piece = chunks // pieces
    me = lax.axis_index("seq")
    core = lax.rem(me, 2)
    y = lax.rem(me // 2, 2)
    z = me // 4
    planes = devices // 4
    partner = me + 1 - 2 * core
    across = me + 2 - 4 * y
    sources = (q_hbm, k_hbm, v_hbm)

    def load_tail(which):
        rows = pl.ds(tokens - RIM, RIM)
        return pltpu.make_async_copy(sources[which].at[rows], tail.at[which], tail_sem.at[which])

    def load(buf, which, c):
        cols = pl.ds(pl.multiple_of(c * chunk, chunk), chunk)
        return pltpu.make_async_copy(sources[which].at[:, cols], buf.at[:, cols], load_sem.at[which, c])

    for which in (1, 2, 0):
        load_tail(which).start()

    @pl.loop(0, chunks)
    def _(c):
        load(k_buf, 1, c).start()
        load(v_buf, 2, c).start()

    barrier = pltpu.get_barrier_semaphore()

    def greet(target):
        pl.semaphore_signal(barrier, inc=1, device_id={"seq": target}, device_id_type=MESH)

    greet(partner)
    greet(across)

    @pl.when(me > 0)
    def _():
        greet(me - 1)

    @pl.when(me < devices - 1)
    def _():
        greet(me + 1)

    @pl.when(z > 0)
    def _():
        greet(me - 4)

    @pl.when(z < planes - 1)
    def _():
        greet(me + 4)

    @pl.loop(0, chunks)
    def _(c):
        load(q_buf, 0, c).start()

    wide_map[...] = jnp.zeros_like(wide_map)
    wide_map[:dim, :dim] = feature_map[...]
    wide_map[dim:, dim:] = feature_map[...]

    @pl.when(me == 0)
    def _():
        halo[...] = jnp.zeros_like(halo)

    @pl.when(z == 0)
    def _():
        @pl.loop(0, chunks)
        def _(c):
            z_in[c] = jnp.zeros(z_in.shape[1:], BF16)

    for which in (1, 2, 0):
        load_tail(which).wait()
        halo_out[which] = tail[which].astype(F32)[RIM - HALO :].astype(BF16)

    edges = [(me > 0), (me < devices - 1), (z > 0), (z < planes - 1)]
    pl.semaphore_wait(barrier, 2 + sum(e.astype(jnp.int32) for e in edges))

    def remote(src, dst, kind, recv_sem, target):
        return pltpu.make_async_remote_copy(
            src_ref=src,
            dst_ref=dst,
            send_sem=send_sem.at[kind],
            recv_sem=recv_sem,
            device_id={"seq": target},
            device_id_type=MESH,
        )

    def halo_copy(which, piece):
        size = width // pieces
        cols = pl.ds(pl.multiple_of(piece * size, size), size)
        return remote(
            halo_out.at[which, :, cols],
            halo.at[which, :, cols],
            0,
            halo_sem.at[which, piece],
            lax.rem(me + 1, devices),
        )

    @pl.when(me < devices - 1)
    def _():
        @pl.loop(0, pieces)
        def _(piece):
            halo_copy(1, piece).start()
            halo_copy(2, piece).start()

        @pl.loop(0, pieces)
        def _(piece):
            halo_copy(0, piece).start()

    def wait_halo(c, which):
        @pl.when((me > 0) & (lax.rem(c, per_piece) == 0))
        def _():
            for w in which:
                halo_copy(w, c // per_piece).wait_recv()

    lead = pl.ds(pl.multiple_of(y * dim, dim), dim)
    other = pl.ds(pl.multiple_of((1 - y) * dim, dim), dim)

    def x_copy(c):
        return remote(x_out.at[c], x_in.at[c], 1, x_sem.at[c], partner)

    def raw_copy(c):
        return remote(raw_out.at[c], raw_in.at[c], 2, raw_sem.at[c], across)

    def z_copy(c):
        return remote(z_out.at[c], z_in.at[c], 3, z_sem.at[c], lax.rem(me + 4, devices))

    def res_copy(c):
        return remote(res_out.at[c], res_in.at[c], 4, res_sem.at[c], across)

    def p_copy(c, h):
        rows = pl.ds(pl.multiple_of(h * dim, dim), dim)
        return remote(p_out.at[c, rows], prefix.at[c, core, rows], 5, p_sem.at[c, h], partner)

    def states(c):
        load(k_buf, 1, c).wait()
        load(v_buf, 2, c).wait()
        wait_halo(c, (1, 2))
        found = []
        for side in range(2):
            turn = 1 - core if side == 0 else core
            col = pl.multiple_of(c * chunk + turn * pair, pair)
            k_rows = short_conv(k_buf, halo, taps, 1, col, pair, wide.at[2 * side])
            v_rows = short_conv(v_buf, halo, taps, 2, col, pair, wide.at[2 * side + 1])
            feat = features(k_rows, wide_map)
            k_feat[:, pl.ds(col, pair)] = feat
            v_conv[:, pl.ds(col, pair)] = v_rows
            both = lax.dot_general(feat, v_rows, (((0,), (0,)), ((), ())), preferred_element_type=F32)
            found.append((both[:dim, :dim], both[dim:, dim:]))
        x_out[c, :dim] = found[0][0].astype(BF16)
        x_out[c, dim:] = found[0][1].astype(BF16)
        own_state[c, :dim] = found[1][0]
        own_state[c, dim:] = found[1][1]
        x_copy(c).start()

    def relay_raw(c):
        x_copy(c).wait_recv()
        raw_out[c] = (own_state[c, other] + x_in[c, other].astype(F32)).astype(BF16)
        raw_copy(c).start()

    def hand_on(c, h, rows, earlier):
        p_out[c, rows] = (earlier + jnp.where(core == 0, own_state[c, rows], 0.0)).astype(BF16)
        p_copy(c, h).start()
        own = earlier + jnp.where(core == 1, x_in[c, rows].astype(F32), 0.0)
        prefix[c, core, rows] = own.astype(BF16)

    def relay_z(c):
        raw_copy(c).wait_recv()

        @pl.when(z > 0)
        def _():
            z_copy(c).wait_recv()

        before = z_in[c].astype(F32)
        chip = own_state[c, lead] + x_in[c, lead].astype(F32)
        far = raw_in[c].astype(F32)
        z_out[c] = (before + chip + far).astype(BF16)

        @pl.when(z < planes - 1)
        def _():
            z_copy(c).start()

        res_out[c] = (before + jnp.where(y == 0, chip, 0.0)).astype(BF16)
        res_copy(c).start()
        hand_on(c, y, lead, before + jnp.where(y == 1, far, 0.0))

    def relay_res(c):
        res_copy(c).wait_recv()
        hand_on(c, 1 - y, other, res_in[c].astype(F32))

    def local_mix(c):
        load(q_buf, 0, c).wait()
        wait_halo(c, (0,))
        row = lax.broadcasted_iota(jnp.int32, (half, half), 0)
        causal = row >= lax.broadcasted_iota(jnp.int32, (half, half), 1)
        for side in range(2):
            col = pl.multiple_of(c * chunk + side * pair, pair)
            q_rows = short_conv(q_buf, halo, taps, 0, col, pair, wide.at[side])
            feat = features(q_rows, wide_map)
            q_feat[:, pl.ds(col, pair)] = feat
            for head in range(2):
                cols = pl.ds(pl.multiple_of(col + head * dim, dim), dim)
                scores = lax.dot_general(
                    feat[:, head * dim : (head + 1) * dim],
                    k_feat[:, cols],
                    (((1,), (1,)), ((), ())),
                    preferred_element_type=F32,
                )
                upper = jnp.where(causal, scores[:half, :half], 0.0).astype(BF16)
                left = scores[half:, :half].astype(BF16)
                lower = jnp.where(causal, scores[half:, half:], 0.0).astype(BF16)
                values = v_conv[:, cols]
                mixed[:half, cols] = jnp.dot(upper, values[:half], preferred_element_type=F32)
                mixed[half:, cols] = jnp.dot(
                    jnp.concatenate([left, lower], axis=1), values, preferred_element_type=F32
                )

    def finish(c):
        p_copy(c, 0).wait_recv()
        p_copy(c, 1).wait_recv()
        for head in range(4):
            cols = pl.ds(pl.multiple_of(c * chunk + head * dim, dim), dim)
            state = prefix[c, head // 2, (head % 2) * dim : (head % 2 + 1) * dim]
            rows = mixed[:, cols] + jnp.dot(q_feat[:, cols], state, preferred_element_type=F32)
            scale = lax.rsqrt(jnp.mean(rows * rows, axis=-1, keepdims=True) + 1e-06)
            out_buf[:, cols] = (rows * scale * gain[:, cols]).astype(BF16)

    z_lag = X_LAG + Y_LAG + Z_LAG * z
    res_lag = z_lag + R_LAG
    last_lag = jnp.maximum(res_lag + P_LAG, MIX_LAG)

    def at(step, lag, work):
        c = step - lag

        @pl.when((c >= 0) & (c < chunks))
        def _():
            work(c)

    @pl.loop(0, chunks + last_lag)
    def _(step):
        at(step, 0, states)
        at(step, X_LAG, relay_raw)
        at(step, z_lag, relay_z)
        at(step, res_lag, relay_res)
        at(step, MIX_LAG, local_mix)
        at(step, last_lag, finish)

    @pl.when(me < devices - 1)
    def _():
        remote(halo_out, halo, 0, halo_sem.at[0, 0], partner).wait_send()

    remote(x_out, x_in, 1, x_sem.at[0], partner).wait_send()
    remote(raw_out, raw_in, 2, raw_sem.at[0], across).wait_send()

    @pl.when(z < planes - 1)
    def _():
        remote(z_out, z_in, 3, z_sem.at[0], partner).wait_send()

    remote(res_out, res_in, 4, res_sem.at[0], across).wait_send()
    remote(p_out, p_out, 5, p_sem.at[0, 0], partner).wait_send()


def on_device(query_seq, key_seq, value_seq, conv_kernel, feature_map, norm_gain):
    tokens, width = query_seq.shape
    dim = feature_map.shape[0]
    devices = lax.axis_size("seq")
    chunks = width // (4 * dim)
    pieces = chunks // 3 if chunks % 3 == 0 else chunks
    rows = pltpu.VMEM((tokens, width), BF16)
    duo = pltpu.VMEM((chunks, 2 * dim, dim), BF16)
    solo = pltpu.VMEM((chunks, dim, dim), BF16)
    dma = pltpu.SemaphoreType.DMA
    hbm = pl.BlockSpec(memory_space=pl.ANY)
    vmem = pl.BlockSpec(memory_space=pltpu.VMEM)
    return pl.pallas_call(
        functools.partial(kernel, devices),
        out_shape=pltpu.MemorySpace.VMEM((tokens, width), BF16),
        in_specs=[hbm, hbm, hbm, vmem, vmem, vmem],
        out_specs=vmem,
        scratch_shapes=[
            rows,
            rows,
            rows,
            pltpu.VMEM((3, RIM, width), BF16),
            pltpu.VMEM((3, HALO, width), BF16),
            pltpu.VMEM((3, HALO, width), BF16),
            pltpu.VMEM((4, 2, RIM + tokens, LANES), F32),
            pltpu.VMEM((2 * dim, 2 * dim), BF16),
            rows,
            rows,
            rows,
            pltpu.VMEM((tokens, width), F32),
            pltpu.VMEM((chunks, 2 * dim, dim), F32),
            duo,
            duo,
            solo,
            solo,
            solo,
            solo,
            solo,
            solo,
            duo,
            pltpu.VMEM((chunks, 2, 2 * dim, dim), BF16),
            dma((3, chunks)),
            dma((3,)),
            dma((6,)),
            dma((3, pieces)),
            dma((chunks,)),
            dma((chunks,)),
            dma((chunks,)),
            dma((chunks,)),
            dma((chunks, 2)),
        ],
        compiler_params=pltpu.CompilerParams(
            collective_id=0, has_side_effects=True, vmem_limit_bytes=60 * 1024 * 1024
        ),
        name="layer",
    )(query_seq, key_seq, value_seq, conv_kernel, feature_map, norm_gain.reshape(1, width))


def solution(mesh):
    split = P(("groups", "seq"), None)
    return jax.shard_map(
        on_device,
        mesh=mesh,
        in_specs=(split, split, split, P(), P(), P()),
        out_specs=split,
        check_vma=False,
    )
```

```python
import functools

import jax
import jax.numpy as jnp
from jax import lax
from jax.experimental import pallas as pl
from jax.experimental.pallas import tpu as pltpu
from jax.sharding import PartitionSpec as P

MESH = pl.DeviceIdType.MESH
F32 = jnp.float32
BF16 = jnp.bfloat16
RIM = 8
HALO = 4
LANES = 128
X_LAG = 2
Y_LAG = 4
Z_LAG = 4
R_LAG = 4
P_LAG = 2
MIX_LAG = 12


def short_conv(buf, halo, taps, which, col, width, wide):
    tap_count = taps.shape[1]
    length = buf.shape[0]
    out = []
    for j in range(width // LANES):
        lanes = pl.ds(pl.multiple_of(col + j * LANES, LANES), LANES)
        tall = wide.at[j]
        tap_rows = taps[which, :, lanes].astype(F32)
        tall[RIM - HALO : RIM] = halo[which, :, lanes].astype(F32)
        rows = buf[:, lanes].astype(F32)
        tall[RIM:] = rows
        total = tap_rows[0:1] * rows
        for offset in range(1, tap_count):
            total = total + tap_rows[offset : offset + 1] * tall[RIM - offset : RIM - offset + length]
        out.append(total.astype(BF16))
    return jnp.concatenate(out, axis=1)


def features(conv_rows, wide_map):
    projected = jnp.dot(conv_rows, wide_map[...], preferred_element_type=F32)
    return jnp.where(projected > 0, projected + 1.0, jnp.exp(projected)).astype(BF16)


def kernel(
    devices,
    q_hbm,
    k_hbm,
    v_hbm,
    taps_hbm,
    map_hbm,
    gain_hbm,
    out_buf,
    q_buf,
    k_buf,
    v_buf,
    taps,
    feature_map,
    gain,
    tail,
    halo_out,
    halo,
    wide,
    wide_map,
    q_feat,
    k_feat,
    v_conv,
    mixed,
    weights,
    own_state,
    x_out,
    x_in,
    raw_out,
    raw_in,
    z_out,
    z_in,
    res_out,
    res_in,
    p_out,
    prefix,
    load_sem,
    aux_sem,
    tail_sem,
    send_sem,
    halo_sem,
    x_sem,
    raw_sem,
    z_sem,
    res_sem,
    p_sem,
):
    tokens, width = q_buf.shape
    half = tokens // 2
    dim = feature_map.shape[0]
    pair = 2 * dim
    chunk = 2 * pair
    chunks = width // chunk
    pieces = halo_sem.shape[1]
    per_piece = chunks // pieces
    me = lax.axis_index("seq")
    core = lax.rem(me, 2)
    y = lax.rem(me // 2, 2)
    z = me // 4
    planes = devices // 4
    partner = me + 1 - 2 * core
    across = me + 2 - 4 * y
    sources = (q_hbm, k_hbm, v_hbm)

    def load_tail(which):
        rows = pl.ds(tokens - RIM, RIM)
        return pltpu.make_async_copy(sources[which].at[rows], tail.at[which], tail_sem.at[which])

    def load(buf, which, c):
        cols = pl.ds(pl.multiple_of(c * chunk, chunk), chunk)
        return pltpu.make_async_copy(sources[which].at[:, cols], buf.at[:, cols], load_sem.at[which, c])

    small = [
        pltpu.make_async_copy(src, dst, aux_sem.at[n])
        for n, (src, dst) in enumerate(((taps_hbm, taps), (map_hbm, feature_map), (gain_hbm, gain)))
    ]
    barrier = pltpu.get_barrier_semaphore()

    def greet(target):
        pl.semaphore_signal(barrier, inc=1, device_id={"seq": target}, device_id_type=MESH)

    greet(partner)
    greet(across)

    @pl.when(me > 0)
    def _():
        greet(me - 1)

    @pl.when(me < devices - 1)
    def _():
        greet(me + 1)

    @pl.when(z > 0)
    def _():
        greet(me - 4)

    @pl.when(z < planes - 1)
    def _():
        greet(me + 4)

    load_tail(1).start()
    load_tail(2).start()
    small[0].start()
    small[1].start()

    @pl.loop(0, chunks)
    def _(c):
        load(k_buf, 1, c).start()
        load(v_buf, 2, c).start()

    load_tail(0).start()
    small[2].start()

    @pl.loop(0, chunks)
    def _(c):
        load(q_buf, 0, c).start()

    wide_map[...] = jnp.zeros_like(wide_map)

    @pl.when(me == 0)
    def _():
        halo[...] = jnp.zeros_like(halo)

    @pl.when(z == 0)
    def _():
        @pl.loop(0, chunks)
        def _(c):
            z_in[c] = jnp.zeros(z_in.shape[1:], BF16)

    for which in (1, 2, 0):
        load_tail(which).wait()
        halo_out[which] = tail[which].astype(F32)[RIM - HALO :].astype(BF16)

    small[0].wait()
    small[1].wait()
    wide_map[:dim, :dim] = feature_map[...]
    wide_map[dim:, dim:] = feature_map[...]

    edges = [(me > 0), (me < devices - 1), (z > 0), (z < planes - 1)]
    pl.semaphore_wait(barrier, 2 + sum(e.astype(jnp.int32) for e in edges))

    def remote(src, dst, kind, recv_sem, target):
        return pltpu.make_async_remote_copy(
            src_ref=src,
            dst_ref=dst,
            send_sem=send_sem.at[kind],
            recv_sem=recv_sem,
            device_id={"seq": target},
            device_id_type=MESH,
        )

    def halo_copy(which, piece):
        size = width // pieces
        cols = pl.ds(pl.multiple_of(piece * size, size), size)
        return remote(
            halo_out.at[which, :, cols],
            halo.at[which, :, cols],
            0,
            halo_sem.at[which, piece],
            lax.rem(me + 1, devices),
        )

    @pl.when(me < devices - 1)
    def _():
        @pl.loop(0, pieces)
        def _(piece):
            halo_copy(1, piece).start()
            halo_copy(2, piece).start()

        @pl.loop(0, pieces)
        def _(piece):
            halo_copy(0, piece).start()

    def wait_halo(c, which):
        @pl.when((me > 0) & (lax.rem(c, per_piece) == 0))
        def _():
            for w in which:
                halo_copy(w, c // per_piece).wait_recv()

    lead = pl.ds(pl.multiple_of(y * dim, dim), dim)
    other = pl.ds(pl.multiple_of((1 - y) * dim, dim), dim)

    def x_copy(c):
        return remote(x_out.at[c], x_in.at[c], 1, x_sem.at[c], partner)

    def raw_copy(c):
        return remote(raw_out.at[c], raw_in.at[c], 2, raw_sem.at[c], across)

    def z_copy(c):
        return remote(z_out.at[c], z_in.at[c], 3, z_sem.at[c], lax.rem(me + 4, devices))

    def res_copy(c):
        return remote(res_out.at[c], res_in.at[c], 4, res_sem.at[c], across)

    def p_copy(c, h):
        rows = pl.ds(pl.multiple_of(h * dim, dim), dim)
        return remote(p_out.at[c, rows], prefix.at[c, core, rows], 5, p_sem.at[c, h], partner)

    def pair_state(feat, v_rows):
        both = lax.dot_general(feat, v_rows, (((0,), (0,)), ((), ())), preferred_element_type=F32)
        return both[:dim, :dim], both[dim:, dim:]

    def keep_own(c):
        cols = pl.ds(pl.multiple_of(c * chunk + core * pair, pair), pair)
        first, second = pair_state(k_feat[:, cols], v_conv[:, cols])
        own_state[c, :dim] = first
        own_state[c, dim:] = second

    def states(c):
        load(k_buf, 1, c).wait()
        load(v_buf, 2, c).wait()
        wait_halo(c, (1, 2))
        keep_own(jnp.maximum(c - 1, 0))
        for side in range(2):
            turn = 1 - core if side == 0 else core
            col = pl.multiple_of(c * chunk + turn * pair, pair)
            k_rows = short_conv(k_buf, halo, taps, 1, col, pair, wide.at[2 * side])
            feat = features(k_rows, wide_map)
            v_rows = short_conv(v_buf, halo, taps, 2, col, pair, wide.at[2 * side + 1])
            k_feat[:, pl.ds(col, pair)] = feat
            v_conv[:, pl.ds(col, pair)] = v_rows
            if side == 0:
                first, second = pair_state(feat, v_rows)
                x_out[c, :dim] = first.astype(BF16)
                x_out[c, dim:] = second.astype(BF16)
        x_copy(c).start()

    def relay_raw(c):
        x_copy(c).wait_recv()
        raw_out[c] = (own_state[c, other] + x_in[c, other].astype(F32)).astype(BF16)
        raw_copy(c).start()

    def hand_on(c, h, rows, earlier):
        p_out[c, rows] = (earlier + jnp.where(core == 0, own_state[c, rows], 0.0)).astype(BF16)
        p_copy(c, h).start()
        own = earlier + jnp.where(core == 1, x_in[c, rows].astype(F32), 0.0)
        prefix[c, core, rows] = own.astype(BF16)

    def relay_z(c):
        raw_copy(c).wait_recv()

        @pl.when(z > 0)
        def _():
            z_copy(c).wait_recv()

        before = z_in[c].astype(F32)
        chip = own_state[c, lead] + x_in[c, lead].astype(F32)
        far = raw_in[c].astype(F32)
        z_out[c] = (before + chip + far).astype(BF16)

        @pl.when(z < planes - 1)
        def _():
            z_copy(c).start()

        res_out[c] = (before + jnp.where(y == 0, chip, 0.0)).astype(BF16)
        hand_on(c, y, lead, before + jnp.where(y == 1, far, 0.0))

    def send_res(c):
        res_copy(c).start()

    def relay_res(c):
        res_copy(c).wait_recv()
        hand_on(c, 1 - y, other, res_in[c].astype(F32))

    def mix_values(c):
        for head in range(4):
            cols = pl.ds(pl.multiple_of(c * chunk + head * dim, dim), dim)
            values = v_conv[:, cols]
            mixed[:half, cols] = jnp.dot(weights[head, :half, :half], values[:half], preferred_element_type=F32)
            mixed[half:, cols] = jnp.dot(weights[head, half:], values, preferred_element_type=F32)

    def query(c):
        for side in range(2):
            col = pl.multiple_of(c * chunk + side * pair, pair)
            q_rows = short_conv(q_buf, halo, taps, 0, col, pair, wide.at[side])
            q_feat[:, pl.ds(col, pair)] = features(q_rows, wide_map)

    def mix_scores(c):
        row = lax.broadcasted_iota(jnp.int32, (half, half), 0)
        causal = row >= lax.broadcasted_iota(jnp.int32, (half, half), 1)
        for head in range(4):
            cols = pl.ds(pl.multiple_of(c * chunk + head * dim, dim), dim)
            scores = lax.dot_general(
                q_feat[:, cols], k_feat[:, cols], (((1,), (1,)), ((), ())), preferred_element_type=F32
            )
            place = weights.at[head]
            place[:half, :half] = jnp.where(causal, scores[:half, :half], 0.0).astype(BF16)
            place[half:, :half] = scores[half:, :half].astype(BF16)
            place[half:, half:] = jnp.where(causal, scores[half:, half:], 0.0).astype(BF16)

    def await_query(c):
        @pl.when(c < chunks)
        def _():
            load(q_buf, 0, c).wait()
            wait_halo(c, (0,))

    def local_mix(c):
        await_query(c + 1)
        mix_values(jnp.maximum(c - 1, 0))
        mix_scores(c)
        query(jnp.minimum(c + 1, chunks - 1))

    def finish(c):
        p_copy(c, 0).wait_recv()
        p_copy(c, 1).wait_recv()
        for head in range(4):
            cols = pl.ds(pl.multiple_of(c * chunk + head * dim, dim), dim)
            state = prefix[c, head // 2, (head % 2) * dim : (head % 2 + 1) * dim]
            rows = mixed[:, cols] + jnp.dot(q_feat[:, cols], state, preferred_element_type=F32)
            scale = lax.rsqrt(jnp.mean(rows * rows, axis=-1, keepdims=True) + 1e-06)
            out_buf[:, cols] = (rows * scale * gain[:, cols]).astype(BF16)

    z_lag = X_LAG + Y_LAG + Z_LAG * z
    send_lag = jnp.maximum(z_lag, chunks + X_LAG)
    res_lag = send_lag + R_LAG
    last_lag = jnp.maximum(res_lag + P_LAG, MIX_LAG + 1)

    def at(step, lag, work):
        c = step - lag

        @pl.when((c >= 0) & (c < chunks))
        def _():
            work(c)

    @pl.loop(0, chunks + last_lag)
    def _(step):
        at(step, 0, states)
        @pl.when(step == chunks)
        def _():
            keep_own(chunks - 1)

        at(step, X_LAG, relay_raw)
        at(step, z_lag, relay_z)
        at(step, send_lag, send_res)
        at(step, res_lag, relay_res)
        @pl.when(step == MIX_LAG - 1)
        def _():
            small[2].wait()
            await_query(0)
            query(0)

        at(step, MIX_LAG, local_mix)

        @pl.when(step == MIX_LAG + chunks)
        def _():
            mix_values(chunks - 1)

        at(step, last_lag, finish)

    @pl.when(me < devices - 1)
    def _():
        remote(halo_out, halo, 0, halo_sem.at[0, 0], partner).wait_send()

    remote(x_out, x_in, 1, x_sem.at[0], partner).wait_send()
    remote(raw_out, raw_in, 2, raw_sem.at[0], across).wait_send()

    @pl.when(z < planes - 1)
    def _():
        remote(z_out, z_in, 3, z_sem.at[0], partner).wait_send()

    remote(res_out, res_in, 4, res_sem.at[0], across).wait_send()
    remote(p_out, p_out, 5, p_sem.at[0, 0], partner).wait_send()


def on_device(query_seq, key_seq, value_seq, conv_kernel, feature_map, norm_gain):
    tokens, width = query_seq.shape
    dim = feature_map.shape[0]
    devices = lax.axis_size("seq")
    chunks = width // (4 * dim)
    pieces = chunks // 3 if chunks % 3 == 0 else chunks
    rows = pltpu.VMEM((tokens, width), BF16)
    duo = pltpu.VMEM((chunks, 2 * dim, dim), BF16)
    solo = pltpu.VMEM((chunks, dim, dim), BF16)
    dma = pltpu.SemaphoreType.DMA
    hbm = pl.BlockSpec(memory_space=pl.ANY)
    vmem = pl.BlockSpec(memory_space=pltpu.VMEM)
    return pl.pallas_call(
        functools.partial(kernel, devices),
        out_shape=pltpu.MemorySpace.VMEM((tokens, width), BF16),
        in_specs=[hbm] * 6,
        out_specs=vmem,
        scratch_shapes=[
            rows,
            rows,
            rows,
            pltpu.VMEM(conv_kernel.shape, BF16),
            pltpu.VMEM(feature_map.shape, BF16),
            pltpu.VMEM((1, width), F32),
            pltpu.VMEM((3, RIM, width), BF16),
            pltpu.VMEM((3, HALO, width), BF16),
            pltpu.VMEM((3, HALO, width), BF16),
            pltpu.VMEM((4, 2, RIM + tokens, LANES), F32),
            pltpu.VMEM((2 * dim, 2 * dim), BF16),
            rows,
            rows,
            rows,
            pltpu.VMEM((tokens, width), F32),
            pltpu.VMEM((4, tokens, tokens), BF16),
            pltpu.VMEM((chunks, 2 * dim, dim), F32),
            duo,
            duo,
            solo,
            solo,
            solo,
            solo,
            solo,
            solo,
            duo,
            pltpu.VMEM((chunks, 2, 2 * dim, dim), BF16),
            dma((3, chunks)),
            dma((3,)),
            dma((3,)),
            dma((6,)),
            dma((3, pieces)),
            dma((chunks,)),
            dma((chunks,)),
            dma((chunks,)),
            dma((chunks,)),
            dma((chunks, 2)),
        ],
        compiler_params=pltpu.CompilerParams(
            collective_id=0, has_side_effects=True, vmem_limit_bytes=60 * 1024 * 1024
        ),
        name="layer",
    )(query_seq, key_seq, value_seq, conv_kernel, feature_map, norm_gain.reshape(1, width))


def solution(mesh):
    split = P(("groups", "seq"), None)
    return jax.shard_map(
        on_device,
        mesh=mesh,
        in_specs=(split, split, split, P(), P(), P()),
        out_specs=split,
        check_vma=False,
    )
```

```python
import functools

import jax
import jax.numpy as jnp
from jax import lax
from jax.experimental import pallas as pl
from jax.experimental.pallas import tpu as pltpu
from jax.sharding import PartitionSpec as P

MESH = pl.DeviceIdType.MESH
F32 = jnp.float32
BF16 = jnp.bfloat16
RIM = 8
HALO = 4
LANES = 128
X_LAG = 2
Y_LAG = 4
Z_LAG = 3
R_LAG = 3
P_LAG = 2
MIX_LAG = 11
LAST_MIX_LAG = 9
TAIL = 2


def short_conv(buf, halo, taps, which, col, width, wide):
    tap_count = taps.shape[1]
    length = buf.shape[0]
    out = []
    for j in range(width // LANES):
        lanes = pl.ds(pl.multiple_of(col + j * LANES, LANES), LANES)
        tall = wide.at[j]
        tap_rows = taps[which, :, lanes].astype(F32)
        tall[RIM - HALO : RIM] = halo[which, :, lanes].astype(F32)
        rows = buf[:, lanes].astype(F32)
        tall[RIM:] = rows
        total = tap_rows[0:1] * rows
        for offset in range(1, tap_count):
            total = total + tap_rows[offset : offset + 1] * tall[RIM - offset : RIM - offset + length]
        out.append(total.astype(BF16))
    return jnp.concatenate(out, axis=1)


def features(conv_rows, wide_map):
    projected = jnp.dot(conv_rows, wide_map[...], preferred_element_type=F32)
    return jnp.where(projected > 0, projected + 1.0, jnp.exp(projected)).astype(BF16)


def put_pair(buf, first, rows):
    dim = buf.shape[2]
    buf[first] = rows[:, :dim]
    buf[first + 1] = rows[:, dim:]


def get_pair(buf, first):
    return jnp.concatenate([buf[first], buf[first + 1]], axis=1)


def fill_average(average):
    dim = average.shape[0] // 2
    average[...] = jnp.zeros_like(average)
    average[:dim, :dim] = jnp.full((dim, dim), 1.0 / dim, BF16)
    average[dim:, dim:] = jnp.full((dim, dim), 1.0 / dim, BF16)


def normalize(c, out, first, mixed, q_feat, prefix, gain, total, squares, average):
    pair = average.shape[0]
    spans = [pl.ds(pl.multiple_of((2 * c + side) * pair, pair), pair) for side in range(2)]
    for side in range(2):
        query = get_pair(q_feat, 4 * c + 2 * side)
        rows = mixed[:, spans[side]] + jnp.dot(query, prefix[c, side], preferred_element_type=F32)
        total[side] = rows
        squares[side] = (rows * rows).astype(BF16)
    for side in range(2):
        mean = jnp.dot(squares[side], average[...], preferred_element_type=F32)
        done = (total[side] * lax.rsqrt(mean + 1e-06) * gain[:, spans[side]]).astype(BF16)
        put_pair(out, first + 2 * side, done)


def kernel(
    devices,
    q_hbm,
    k_hbm,
    v_hbm,
    taps_hbm,
    map_hbm,
    gain_hbm,
    out_buf,
    mixed,
    q_feat,
    prefix,
    gain,
    q_buf,
    k_buf,
    v_buf,
    taps,
    feature_map,
    tail,
    halo_out,
    halo,
    wide,
    wide_map,
    q_stage,
    k_feat,
    v_conv,
    weights,
    total,
    squares,
    average,
    own_state,
    x_out,
    x_in,
    raw_out,
    raw_in,
    z_out,
    z_in,
    res_out,
    res_in,
    p_out,
    load_sem,
    aux_sem,
    tail_sem,
    send_sem,
    halo_sem,
    x_sem,
    raw_sem,
    z_sem,
    res_sem,
    p_sem,
):
    tokens, width = q_buf.shape
    half = tokens // 2
    dim = feature_map.shape[0]
    pair = 2 * dim
    chunk = 2 * pair
    chunks = width // chunk
    me = lax.axis_index("seq")
    core = lax.rem(me, 2)
    y = lax.rem(me // 2, 2)
    z = me // 4
    planes = devices // 4
    partner = me + 1 - 2 * core
    across = me + 2 - 4 * y
    sources = (q_hbm, k_hbm, v_hbm)

    def load_tail(which):
        rows = pl.ds(tokens - RIM, RIM)
        return pltpu.make_async_copy(sources[which].at[rows], tail.at[which], tail_sem.at[which])

    def load(buf, which, c):
        cols = pl.ds(pl.multiple_of(c * chunk, chunk), chunk)
        return pltpu.make_async_copy(sources[which].at[:, cols], buf.at[:, cols], load_sem.at[which, c])

    small = [
        pltpu.make_async_copy(src, dst, aux_sem.at[n])
        for n, (src, dst) in enumerate(((taps_hbm, taps), (map_hbm, feature_map), (gain_hbm, gain)))
    ]
    barrier = pltpu.get_barrier_semaphore()

    def greet(target):
        pl.semaphore_signal(barrier, inc=1, device_id={"seq": target}, device_id_type=MESH)

    greet(partner)
    greet(across)

    @pl.when(me > 0)
    def _():
        greet(me - 1)

    @pl.when(me < devices - 1)
    def _():
        greet(me + 1)

    @pl.when(z > 0)
    def _():
        greet(me - 4)

    @pl.when(z < planes - 1)
    def _():
        greet(me + 4)

    load_tail(1).start()
    load_tail(2).start()
    small[0].start()
    small[1].start()

    def load_pair(c):
        load(k_buf, 1, c).start()
        load(v_buf, 2, c).start()

    load_pair(0)
    load_pair(1)

    wide_map[...] = jnp.zeros_like(wide_map)
    fill_average(average)

    @pl.when(me == 0)
    def _():
        halo[...] = jnp.zeros_like(halo)

    @pl.when(z == 0)
    def _():
        @pl.loop(0, chunks)
        def _(c):
            z_in[c] = jnp.zeros(z_in.shape[1:], BF16)

    def ready_tail(which):
        load_tail(which).wait()
        halo_out[which] = tail[which].astype(F32)[RIM - HALO :].astype(BF16)

    ready_tail(1)
    ready_tail(2)
    small[0].wait()
    small[1].wait()
    wide_map[:dim, :dim] = feature_map[...]
    wide_map[dim:, dim:] = feature_map[...]

    edges = [(me > 0), (me < devices - 1), (z > 0), (z < planes - 1)]
    pl.semaphore_wait(barrier, 2 + sum(e.astype(jnp.int32) for e in edges))

    def remote(src, dst, kind, recv_sem, target):
        return pltpu.make_async_remote_copy(
            src_ref=src,
            dst_ref=dst,
            send_sem=send_sem.at[kind],
            recv_sem=recv_sem,
            device_id={"seq": target},
            device_id_type=MESH,
        )

    def halo_copy(which, piece):
        cols = pl.ds(0, chunk) if piece == 0 else pl.ds(chunk, width - chunk)
        return remote(
            halo_out.at[which, :, cols],
            halo.at[which, :, cols],
            0,
            halo_sem.at[which, piece],
            lax.rem(me + 1, devices),
        )

    @pl.when(me < devices - 1)
    def _():
        for piece in range(2):
            for which in (1, 2):
                halo_copy(which, piece).start()

    load_tail(0).start()
    small[2].start()

    @pl.loop(2, chunks)
    def _(c):
        load_pair(c)

    @pl.loop(0, chunks)
    def _(c):
        load(q_buf, 0, c).start()

    @pl.loop(0, chunks)
    def _(c):
        blank = jnp.zeros((dim, dim), BF16)
        for side in range(2):
            prefix[c, side, :dim, dim:] = blank
            prefix[c, side, dim:, :dim] = blank

    ready_tail(0)

    @pl.when(me < devices - 1)
    def _():
        for piece in range(2):
            halo_copy(0, piece).start()

    def wait_halo(c, which):
        for piece in range(2):

            @pl.when((me > 0) & (c == piece))
            def _():
                for w in which:
                    halo_copy(w, piece).wait_recv()

    lead = pl.ds(pl.multiple_of(y * dim, dim), dim)
    other = pl.ds(pl.multiple_of((1 - y) * dim, dim), dim)

    def x_copy(c):
        return remote(x_out.at[c], x_in.at[c], 1, x_sem.at[c], partner)

    def raw_copy(c):
        return remote(raw_out.at[c], raw_in.at[c], 2, raw_sem.at[c], across)

    def z_copy(c):
        return remote(z_out.at[c], z_in.at[c], 3, z_sem.at[c], lax.rem(me + 4, devices))

    def res_copy(c):
        return remote(res_out.at[c], res_in.at[c], 4, res_sem.at[c], across)

    def p_copy(c, h):
        rows = pl.ds(pl.multiple_of(h * dim, dim), dim)
        return remote(p_out.at[c, rows], prefix.at[c, core, rows, rows], 5, p_sem.at[c, h], partner)

    def pair_state(feat, v_rows):
        both = lax.dot_general(feat, v_rows, (((0,), (0,)), ((), ())), preferred_element_type=F32)
        return both[:dim, :dim], both[dim:, dim:]

    def keep_own(c):
        first_head = 4 * c + 2 * core
        first, second = pair_state(get_pair(k_feat, first_head), get_pair(v_conv, first_head))
        own_state[c, :dim] = first
        own_state[c, dim:] = second

    def states(c):
        load(k_buf, 1, c).wait()
        load(v_buf, 2, c).wait()
        wait_halo(c, (1, 2))
        keep_own(jnp.maximum(c - 1, 0))
        turns = (1 - core, core)
        heads = [4 * c + 2 * turn for turn in turns]
        cols = [pl.multiple_of(c * chunk + turn * pair, pair) for turn in turns]

        def key_rows(side):
            return short_conv(k_buf, halo, taps, 1, cols[side], pair, wide.at[2 * side])

        def value_rows(side):
            return short_conv(v_buf, halo, taps, 2, cols[side], pair, wide.at[2 * side + 1])

        key_0 = key_rows(0)
        feat_0 = features(key_0, wide_map)
        key_1 = key_rows(1)
        put_pair(k_feat, heads[0], feat_0)
        values_0 = value_rows(0)
        put_pair(v_conv, heads[0], values_0)
        put_pair(k_feat, heads[1], features(key_1, wide_map))
        first, second = pair_state(feat_0, values_0)
        put_pair(v_conv, heads[1], value_rows(1))
        x_out[c, :dim] = first.astype(BF16)
        x_out[c, dim:] = second.astype(BF16)
        x_copy(c).start()

    def relay_raw(c):
        x_copy(c).wait_recv()
        raw_out[c] = (own_state[c, other] + x_in[c, other].astype(F32)).astype(BF16)
        raw_copy(c).start()

    def hand_on(c, h, rows, earlier):
        p_out[c, rows] = (earlier + jnp.where(core == 0, own_state[c, rows], 0.0)).astype(BF16)
        p_copy(c, h).start()
        own = earlier + jnp.where(core == 1, x_in[c, rows].astype(F32), 0.0)
        prefix[c, core, rows, rows] = own.astype(BF16)

    z_lag = X_LAG + Y_LAG + Z_LAG * z
    raw_end = chunks + X_LAG

    def relay_z(c):
        raw_copy(c).wait_recv()

        @pl.when(z > 0)
        def _():
            z_copy(c).wait_recv()

        before = z_in[c].astype(F32)
        chip = own_state[c, lead] + x_in[c, lead].astype(F32)
        far = raw_in[c].astype(F32)
        z_out[c] = (before + chip + far).astype(BF16)

        @pl.when(z < planes - 1)
        def _():
            z_copy(c).start()

        res_out[c] = (before + jnp.where(y == 0, chip, 0.0)).astype(BF16)

        @pl.when(c + z_lag >= raw_end)
        def _():
            res_copy(c).start()

        hand_on(c, y, lead, before + jnp.where(y == 1, far, 0.0))

    def relay_res(c):
        res_copy(c).wait_recv()
        hand_on(c, 1 - y, other, res_in[c].astype(F32))

    def mix_values(c, head):
        cols = pl.ds(pl.multiple_of(c * chunk + head * dim, dim), dim)
        values = v_conv[4 * c + head]
        mixed[:half, cols] = jnp.dot(weights[head, :half, :half], values[:half], preferred_element_type=F32)
        mixed[half:, cols] = jnp.dot(weights[head, half:], values, preferred_element_type=F32)

    def query_rows(c, side):
        return short_conv(q_buf, halo, taps, 0, c * chunk + side * pair, pair, wide.at[side])

    def query_feat(c, side, rows):
        feat = features(rows, wide_map)
        put_pair(q_stage, 2 * side, feat)
        put_pair(q_feat, 4 * c + 2 * side, feat)

    def mix_scores(c, head):
        row = lax.broadcasted_iota(jnp.int32, (half, half), 0)
        causal = row >= lax.broadcasted_iota(jnp.int32, (half, half), 1)
        scores = lax.dot_general(
            q_stage[head],
            k_feat[4 * c + head],
            (((1,), (1,)), ((), ())),
            preferred_element_type=F32,
        )
        place = weights.at[head]
        place[:half, :half] = jnp.where(causal, scores[:half, :half], 0.0).astype(BF16)
        place[half:, :half] = scores[half:, :half].astype(BF16)
        place[half:, half:] = jnp.where(causal, scores[half:, half:], 0.0).astype(BF16)

    def await_query(c):
        @pl.when(c < chunks)
        def _():
            load(q_buf, 0, c).wait()
            wait_halo(c, (0,))

    def local_mix(c):
        await_query(c + 1)
        last = jnp.maximum(c - 1, 0)
        after = jnp.minimum(c + 1, chunks - 1)
        for side in range(2):
            rows = query_rows(after, side)
            mix_values(last, 2 * side)
            mix_values(last, 2 * side + 1)
            mix_scores(c, 2 * side)
            mix_scores(c, 2 * side + 1)
            query_feat(after, side, rows)

    def finish(c):
        p_copy(c, 0).wait_recv()
        p_copy(c, 1).wait_recv()

        @pl.when(c < chunks - TAIL)
        def _():
            normalize(c, out_buf, 4 * c, mixed, q_feat, prefix, gain, total, squares, average)

    res_lag = jnp.maximum(z_lag, raw_end) + R_LAG
    mix_lag = jnp.where(z == planes - 1, LAST_MIX_LAG, MIX_LAG)
    last_lag = jnp.maximum(res_lag + P_LAG, mix_lag + 1)

    def at(step, lag, work):
        c = step - lag

        @pl.when((c >= 0) & (c < chunks))
        def _():
            work(c)

    @pl.loop(0, chunks + last_lag)
    def _(step):
        at(step, 0, states)
        @pl.when(step == chunks)
        def _():
            keep_own(chunks - 1)

        at(step, X_LAG, relay_raw)

        @pl.when(step == raw_end)
        def _():
            @pl.loop(0, jnp.maximum(raw_end - z_lag, 0))
            def _(c):
                res_copy(c).start()

        at(step, z_lag, relay_z)
        at(step, res_lag, relay_res)
        @pl.when(step == mix_lag - 1)
        def _():
            small[2].wait()
            await_query(0)
            for side in range(2):
                query_feat(0, side, query_rows(0, side))

        at(step, mix_lag, local_mix)

        @pl.when(step == mix_lag + chunks)
        def _():
            for head in range(4):
                mix_values(chunks - 1, head)

        at(step, last_lag, finish)

    @pl.when(me < devices - 1)
    def _():
        remote(halo_out, halo, 0, halo_sem.at[0, 0], partner).wait_send()

    remote(x_out, x_in, 1, x_sem.at[0], partner).wait_send()
    remote(raw_out, raw_in, 2, raw_sem.at[0], across).wait_send()

    @pl.when(z < planes - 1)
    def _():
        remote(z_out, z_in, 3, z_sem.at[0], partner).wait_send()

    remote(res_out, res_in, 4, res_sem.at[0], across).wait_send()
    remote(p_out, p_out, 5, p_sem.at[0, 0], partner).wait_send()


def store(done, mixed, q_feat, prefix, gain, out, late, total, squares, average, sem):
    heads, _, dim = done.shape
    chunks = heads // 4
    ready = chunks - TAIL

    def copy(src, h):
        cols = pl.ds(pl.multiple_of(h * dim, dim), dim)
        return pltpu.make_async_copy(src, out.at[:, cols], sem.at[0])

    @pl.loop(0, 4 * ready)
    def _(h):
        copy(done.at[h], h).start()

    fill_average(average)

    @pl.loop(0, TAIL)
    def _(n):
        normalize(ready + n, late, 4 * n, mixed, q_feat, prefix, gain, total, squares, average)
        for h in range(4):
            copy(late.at[4 * n + h], 4 * (ready + n) + h).start()

    pltpu.make_async_copy(out, out, sem.at[0]).wait()


def on_device(query_seq, key_seq, value_seq, conv_kernel, feature_map, norm_gain):
    tokens, width = query_seq.shape
    dim = feature_map.shape[0]
    devices = lax.axis_size("seq")
    chunks = width // (4 * dim)
    rows = pltpu.VMEM((tokens, width), BF16)
    heads = pltpu.VMEM((width // dim, tokens, dim), BF16)
    duo = pltpu.VMEM((chunks, 2 * dim, dim), BF16)
    solo = pltpu.VMEM((chunks, dim, dim), BF16)
    dma = pltpu.SemaphoreType.DMA
    keep = pltpu.MemorySpace.VMEM
    hbm = pl.BlockSpec(memory_space=pl.ANY)
    vmem = pl.BlockSpec(memory_space=pltpu.VMEM)
    parts = pl.pallas_call(
        functools.partial(kernel, devices),
        out_shape=[
            keep((width // dim, tokens, dim), BF16),
            keep((tokens, width), F32),
            keep((width // dim, tokens, dim), BF16),
            keep((chunks, 2, 2 * dim, 2 * dim), BF16),
            keep((1, width), F32),
        ],
        in_specs=[hbm] * 6,
        out_specs=[vmem] * 5,
        scratch_shapes=[
            rows,
            rows,
            rows,
            pltpu.VMEM(conv_kernel.shape, BF16),
            pltpu.VMEM(feature_map.shape, BF16),
            pltpu.VMEM((3, RIM, width), BF16),
            pltpu.VMEM((3, HALO, width), BF16),
            pltpu.VMEM((3, HALO, width), BF16),
            pltpu.VMEM((4, 2, RIM + tokens, LANES), F32),
            pltpu.VMEM((2 * dim, 2 * dim), BF16),
            pltpu.VMEM((4, tokens, dim), BF16),
            heads,
            heads,
            pltpu.VMEM((4, tokens, tokens), BF16),
            pltpu.VMEM((2, tokens, 2 * dim), F32),
            pltpu.VMEM((2, tokens, 2 * dim), BF16),
            pltpu.VMEM((2 * dim, 2 * dim), BF16),
            pltpu.VMEM((chunks, 2 * dim, dim), F32),
            duo,
            duo,
            solo,
            solo,
            solo,
            solo,
            solo,
            solo,
            duo,
            dma((3, chunks)),
            dma((3,)),
            dma((3,)),
            dma((6,)),
            dma((3, 2)),
            dma((chunks,)),
            dma((chunks,)),
            dma((chunks,)),
            dma((chunks,)),
            dma((chunks, 2)),
        ],
        compiler_params=pltpu.CompilerParams(
            collective_id=0, has_side_effects=True, vmem_limit_bytes=40 * 1024 * 1024
        ),
        name="layer",
    )(query_seq, key_seq, value_seq, conv_kernel, feature_map, norm_gain.reshape(1, width))
    return pl.pallas_call(
        store,
        out_shape=jax.ShapeDtypeStruct((tokens, width), BF16),
        in_specs=[vmem] * 5,
        out_specs=hbm,
        scratch_shapes=[
            pltpu.VMEM((4 * TAIL, tokens, dim), BF16),
            pltpu.VMEM((2, tokens, 2 * dim), F32),
            pltpu.VMEM((2, tokens, 2 * dim), BF16),
            pltpu.VMEM((2 * dim, 2 * dim), BF16),
            dma((1,)),
        ],
        compiler_params=pltpu.CompilerParams(vmem_limit_bytes=8 * 1024 * 1024),
        name="store",
    )(*parts)


def solution(mesh):
    split = P(("groups", "seq"), None)
    return jax.shard_map(
        on_device,
        mesh=mesh,
        in_specs=(split, split, split, P(), P(), P()),
        out_specs=split,
        check_vma=False,
    )
```

```python
import functools

import jax
import jax.numpy as jnp
from jax import lax
from jax.experimental import pallas as pl
from jax.experimental.pallas import tpu as pltpu
from jax.sharding import PartitionSpec as P

MESH = pl.DeviceIdType.MESH
F32 = jnp.float32
BF16 = jnp.bfloat16
RIM = 8
HALO = 4
LANES = 128
X_LAG = 2
Y_LAG = 4
Z_LAG = 3
R_LAG = 5
P_LAG = 3
CATCH_ONE = 2
CATCH_TWO = 5
CATCH_PLANE = 3
MIX_LAG = 11
LAST_MIX_LAG = 9
TAIL = 2


def short_conv(buf, halo, taps, which, col, width, wide):
    tap_count = taps.shape[1]
    length = buf.shape[0]
    out = []
    for j in range(width // LANES):
        lanes = pl.ds(pl.multiple_of(col + j * LANES, LANES), LANES)
        tall = wide.at[j]
        tap_rows = taps[which, :, lanes].astype(F32)
        tall[RIM - HALO : RIM] = halo[which, :, lanes].astype(F32)
        rows = buf[:, lanes].astype(F32)
        tall[RIM:] = rows
        total = tap_rows[0:1] * rows
        for offset in range(1, tap_count):
            total = total + tap_rows[offset : offset + 1] * tall[RIM - offset : RIM - offset + length]
        out.append(total.astype(BF16))
    return jnp.concatenate(out, axis=1)


def features(conv_rows, wide_map):
    projected = jnp.dot(conv_rows, wide_map[...], preferred_element_type=F32)
    return jnp.where(projected > 0, projected + 1.0, jnp.exp(projected)).astype(BF16)


def put_pair(buf, first, rows):
    dim = buf.shape[2]
    buf[first] = rows[:, :dim]
    buf[first + 1] = rows[:, dim:]


def get_pair(buf, first):
    return jnp.concatenate([buf[first], buf[first + 1]], axis=1)


def fill_average(average):
    dim = average.shape[0] // 2
    average[...] = jnp.zeros_like(average)
    average[:dim, :dim] = jnp.full((dim, dim), 1.0 / dim, BF16)
    average[dim:, dim:] = jnp.full((dim, dim), 1.0 / dim, BF16)


def normalize(c, out, first, mixed, q_feat, prefix, gain, total, squares, average):
    pair = average.shape[0]
    spans = [pl.ds(pl.multiple_of((2 * c + side) * pair, pair), pair) for side in range(2)]
    for side in range(2):
        query = get_pair(q_feat, 4 * c + 2 * side)
        rows = mixed[:, spans[side]] + jnp.dot(query, prefix[c, side], preferred_element_type=F32)
        total[side] = rows
        squares[side] = (rows * rows).astype(BF16)
    for side in range(2):
        mean = jnp.dot(squares[side], average[...], preferred_element_type=F32)
        done = (total[side] * lax.rsqrt(mean + 1e-06) * gain[:, spans[side]]).astype(BF16)
        put_pair(out, first + 2 * side, done)


def kernel(
    devices,
    q_hbm,
    k_hbm,
    v_hbm,
    taps_hbm,
    map_hbm,
    gain_hbm,
    out_buf,
    mixed,
    q_feat,
    prefix,
    gain,
    q_buf,
    k_buf,
    v_buf,
    taps,
    feature_map,
    tail,
    halo_out,
    halo,
    wide,
    wide_map,
    q_stage,
    k_feat,
    v_conv,
    weights,
    total,
    squares,
    average,
    own_state,
    x_out,
    x_in,
    raw_out,
    raw_in,
    z_out,
    z_in,
    res_out,
    res_in,
    p_out,
    load_sem,
    aux_sem,
    tail_sem,
    send_sem,
    halo_sem,
    x_sem,
    raw_sem,
    z_sem,
    res_sem,
    p_sem,
):
    tokens, width = q_buf.shape
    half = tokens // 2
    dim = feature_map.shape[0]
    pair = 2 * dim
    chunk = 2 * pair
    chunks = width // chunk
    me = lax.axis_index("seq")
    core = lax.rem(me, 2)
    y = lax.rem(me // 2, 2)
    z = me // 4
    planes = devices // 4
    partner = me + 1 - 2 * core
    across = me + 2 - 4 * y
    sources = (q_hbm, k_hbm, v_hbm)

    def load_tail(which):
        rows = pl.ds(tokens - RIM, RIM)
        return pltpu.make_async_copy(sources[which].at[rows], tail.at[which], tail_sem.at[which])

    def load(buf, which, c):
        cols = pl.ds(pl.multiple_of(c * chunk, chunk), chunk)
        return pltpu.make_async_copy(sources[which].at[:, cols], buf.at[:, cols], load_sem.at[which, c])

    small = [
        pltpu.make_async_copy(src, dst, aux_sem.at[n])
        for n, (src, dst) in enumerate(((taps_hbm, taps), (map_hbm, feature_map), (gain_hbm, gain)))
    ]
    barrier = pltpu.get_barrier_semaphore()

    def greet(target):
        pl.semaphore_signal(barrier, inc=1, device_id={"seq": target}, device_id_type=MESH)

    greet(partner)
    greet(across)

    @pl.when(me > 0)
    def _():
        greet(me - 1)

    @pl.when(me < devices - 1)
    def _():
        greet(me + 1)

    @pl.when(z > 0)
    def _():
        greet(me - 4)

    @pl.when(z < planes - 1)
    def _():
        greet(me + 4)

    load_tail(1).start()
    load_tail(2).start()
    small[0].start()
    small[1].start()

    def load_pair(c):
        load(k_buf, 1, c).start()
        load(v_buf, 2, c).start()

    load_pair(0)
    load_pair(1)

    wide_map[...] = jnp.zeros_like(wide_map)
    fill_average(average)

    @pl.when(me == 0)
    def _():
        halo[...] = jnp.zeros_like(halo)

    @pl.when(z == 0)
    def _():
        @pl.loop(0, chunks)
        def _(c):
            z_in[c] = jnp.zeros(z_in.shape[1:], BF16)

    def ready_tail(which):
        load_tail(which).wait()
        halo_out[which] = tail[which].astype(F32)[RIM - HALO :].astype(BF16)

    ready_tail(1)
    ready_tail(2)
    small[0].wait()
    small[1].wait()
    wide_map[:dim, :dim] = feature_map[...]
    wide_map[dim:, dim:] = feature_map[...]

    edges = [(me > 0), (me < devices - 1), (z > 0), (z < planes - 1)]
    pl.semaphore_wait(barrier, 2 + sum(e.astype(jnp.int32) for e in edges))

    def remote(src, dst, kind, recv_sem, target):
        return pltpu.make_async_remote_copy(
            src_ref=src,
            dst_ref=dst,
            send_sem=send_sem.at[kind],
            recv_sem=recv_sem,
            device_id={"seq": target},
            device_id_type=MESH,
        )

    def halo_copy(which, piece):
        cols = pl.ds(0, chunk) if piece == 0 else pl.ds(chunk, width - chunk)
        return remote(
            halo_out.at[which, :, cols],
            halo.at[which, :, cols],
            0,
            halo_sem.at[which, piece],
            lax.rem(me + 1, devices),
        )

    @pl.when(me < devices - 1)
    def _():
        for piece in range(2):
            for which in (1, 2):
                halo_copy(which, piece).start()

    load_tail(0).start()
    small[2].start()

    @pl.loop(2, chunks)
    def _(c):
        load_pair(c)

    @pl.loop(0, chunks)
    def _(c):
        load(q_buf, 0, c).start()

    @pl.loop(0, chunks)
    def _(c):
        blank = jnp.zeros((dim, dim), BF16)
        for side in range(2):
            prefix[c, side, :dim, dim:] = blank
            prefix[c, side, dim:, :dim] = blank

    ready_tail(0)

    @pl.when(me < devices - 1)
    def _():
        for piece in range(2):
            halo_copy(0, piece).start()

    def wait_halo(c, which):
        for piece in range(2):

            @pl.when((me > 0) & (c == piece))
            def _():
                for w in which:
                    halo_copy(w, piece).wait_recv()

    lead = pl.ds(pl.multiple_of(y * dim, dim), dim)
    other = pl.ds(pl.multiple_of((1 - y) * dim, dim), dim)

    def x_copy(c):
        return remote(x_out.at[c], x_in.at[c], 1, x_sem.at[c], partner)

    def raw_copy(c):
        return remote(raw_out.at[c], raw_in.at[c], 2, raw_sem.at[c], across)

    def z_copy(c):
        return remote(z_out.at[c], z_in.at[c], 3, z_sem.at[c], lax.rem(me + 4, devices))

    def res_copy(c):
        return remote(res_out.at[c], res_in.at[c], 4, res_sem.at[c], across)

    def p_copy(c, h):
        rows = pl.ds(pl.multiple_of(h * dim, dim), dim)
        return remote(p_out.at[c, rows], prefix.at[c, core, rows, rows], 5, p_sem.at[c, h], partner)

    def pair_state(feat, v_rows):
        both = lax.dot_general(feat, v_rows, (((0,), (0,)), ((), ())), preferred_element_type=F32)
        return both[:dim, :dim], both[dim:, dim:]

    def keep_own(c):
        first_head = 4 * c + 2 * core
        first, second = pair_state(get_pair(k_feat, first_head), get_pair(v_conv, first_head))
        own_state[c, :dim] = first
        own_state[c, dim:] = second

    def states(c):
        load(k_buf, 1, c).wait()
        load(v_buf, 2, c).wait()
        wait_halo(c, (1, 2))
        keep_own(jnp.maximum(c - 1, 0))
        turns = (1 - core, core)
        heads = [4 * c + 2 * turn for turn in turns]
        cols = [pl.multiple_of(c * chunk + turn * pair, pair) for turn in turns]

        def key_rows(side):
            return short_conv(k_buf, halo, taps, 1, cols[side], pair, wide.at[2 * side])

        def value_rows(side):
            return short_conv(v_buf, halo, taps, 2, cols[side], pair, wide.at[2 * side + 1])

        key_0 = key_rows(0)
        feat_0 = features(key_0, wide_map)
        key_1 = key_rows(1)
        put_pair(k_feat, heads[0], feat_0)
        values_0 = value_rows(0)
        put_pair(v_conv, heads[0], values_0)
        put_pair(k_feat, heads[1], features(key_1, wide_map))
        first, second = pair_state(feat_0, values_0)
        put_pair(v_conv, heads[1], value_rows(1))
        x_out[c, :dim] = first.astype(BF16)
        x_out[c, dim:] = second.astype(BF16)
        x_copy(c).start()

    def relay_raw(c):
        x_copy(c).wait_recv()
        raw_out[c] = (own_state[c, other] + x_in[c, other].astype(F32)).astype(BF16)
        raw_copy(c).start()

    def hand_on(c, h, rows, earlier):
        p_out[c, rows] = (earlier + jnp.where(core == 0, own_state[c, rows], 0.0)).astype(BF16)
        p_copy(c, h).start()
        own = earlier + jnp.where(core == 1, x_in[c, rows].astype(F32), 0.0)
        prefix[c, core, rows, rows] = own.astype(BF16)

    z_lag = X_LAG + Y_LAG + Z_LAG * z
    raw_end = chunks + X_LAG

    def relay_z(c, step):
        raw_copy(c).wait_recv()

        @pl.when(z > 0)
        def _():
            z_copy(c).wait_recv()

        before = z_in[c].astype(F32)
        chip = own_state[c, lead] + x_in[c, lead].astype(F32)
        far = raw_in[c].astype(F32)
        z_out[c] = (before + chip + far).astype(BF16)

        @pl.when(z < planes - 1)
        def _():
            z_copy(c).start()

        res_out[c] = (before + jnp.where(y == 0, chip, 0.0)).astype(BF16)

        @pl.when(step >= raw_end)
        def _():
            res_copy(c).start()

        hand_on(c, y, lead, before + jnp.where(y == 1, far, 0.0))

    def relay_res(c):
        res_copy(c).wait_recv()
        hand_on(c, 1 - y, other, res_in[c].astype(F32))

    def mix_values(c, head):
        cols = pl.ds(pl.multiple_of(c * chunk + head * dim, dim), dim)
        values = v_conv[4 * c + head]
        mixed[:half, cols] = jnp.dot(weights[head, :half, :half], values[:half], preferred_element_type=F32)
        mixed[half:, cols] = jnp.dot(weights[head, half:], values, preferred_element_type=F32)

    def query_rows(c, side):
        return short_conv(q_buf, halo, taps, 0, c * chunk + side * pair, pair, wide.at[side])

    def query_feat(c, side, rows):
        feat = features(rows, wide_map)
        put_pair(q_stage, 2 * side, feat)
        put_pair(q_feat, 4 * c + 2 * side, feat)

    def mix_scores(c, head):
        row = lax.broadcasted_iota(jnp.int32, (half, half), 0)
        causal = row >= lax.broadcasted_iota(jnp.int32, (half, half), 1)
        scores = lax.dot_general(
            q_stage[head],
            k_feat[4 * c + head],
            (((1,), (1,)), ((), ())),
            preferred_element_type=F32,
        )
        place = weights.at[head]
        place[:half, :half] = jnp.where(causal, scores[:half, :half], 0.0).astype(BF16)
        place[half:, :half] = scores[half:, :half].astype(BF16)
        place[half:, half:] = jnp.where(causal, scores[half:, half:], 0.0).astype(BF16)

    def await_query(c):
        @pl.when(c < chunks)
        def _():
            load(q_buf, 0, c).wait()
            wait_halo(c, (0,))

    def local_mix(c):
        await_query(c + 1)
        last = jnp.maximum(c - 1, 0)
        after = jnp.minimum(c + 1, chunks - 1)
        for side in range(2):
            rows = query_rows(after, side)
            mix_values(last, 2 * side)
            mix_values(last, 2 * side + 1)
            mix_scores(c, 2 * side)
            mix_scores(c, 2 * side + 1)
            query_feat(after, side, rows)

    def finish(c):
        p_copy(c, 0).wait_recv()
        p_copy(c, 1).wait_recv()

        @pl.when(c < chunks - TAIL)
        def _():
            normalize(c, out_buf, 4 * c, mixed, q_feat, prefix, gain, total, squares, average)

    mix_lag = jnp.where(z == planes - 1, LAST_MIX_LAG, MIX_LAG)
    catch = 1 + (z >= CATCH_PLANE).astype(jnp.int32)
    last_lag = jnp.maximum(jnp.maximum(raw_end, z_lag - catch) + R_LAG + P_LAG, mix_lag + 1)

    def sums_by(step):
        one = (step >= chunks + CATCH_ONE).astype(jnp.int32)
        two = ((step >= chunks + CATCH_TWO) & (z >= CATCH_PLANE)).astype(jnp.int32)
        return jnp.clip(step - z_lag + 1 + one + two, 0, chunks)

    def results_by(step):
        return jnp.minimum(sums_by(step - R_LAG), jnp.clip(step - raw_end - R_LAG + 1, 0, chunks))

    def finished_by(step):
        return jnp.minimum(results_by(step - P_LAG), jnp.clip(step - mix_lag, 0, chunks))

    def at(step, lag, work):
        c = step - lag

        @pl.when((c >= 0) & (c < chunks))
        def _():
            work(c)

    @pl.loop(0, chunks + last_lag)
    def _(step):
        at(step, 0, states)
        @pl.when(step == chunks)
        def _():
            keep_own(chunks - 1)

        at(step, X_LAG, relay_raw)

        @pl.when(step == raw_end)
        def _():
            @pl.loop(0, sums_by(step - 1))
            def _(c):
                res_copy(c).start()

        @pl.loop(sums_by(step - 1), sums_by(step))
        def _(c):
            relay_z(c, step)

        at(step, jnp.maximum(raw_end, z_lag - catch) + R_LAG, relay_res)
        @pl.when(step == mix_lag - 1)
        def _():
            small[2].wait()
            await_query(0)
            for side in range(2):
                query_feat(0, side, query_rows(0, side))

        at(step, mix_lag, local_mix)

        @pl.when(step == mix_lag + chunks)
        def _():
            for head in range(4):
                mix_values(chunks - 1, head)

        at(step, last_lag, finish)

    @pl.when(me < devices - 1)
    def _():
        remote(halo_out, halo, 0, halo_sem.at[0, 0], partner).wait_send()

    remote(x_out, x_in, 1, x_sem.at[0], partner).wait_send()
    remote(raw_out, raw_in, 2, raw_sem.at[0], across).wait_send()

    @pl.when(z < planes - 1)
    def _():
        remote(z_out, z_in, 3, z_sem.at[0], partner).wait_send()

    remote(res_out, res_in, 4, res_sem.at[0], across).wait_send()
    remote(p_out, p_out, 5, p_sem.at[0, 0], partner).wait_send()


def store(done, mixed, q_feat, prefix, gain, out, late, total, squares, average, sem):
    heads, _, dim = done.shape
    chunks = heads // 4
    ready = chunks - TAIL

    def copy(src, h):
        cols = pl.ds(pl.multiple_of(h * dim, dim), dim)
        return pltpu.make_async_copy(src, out.at[:, cols], sem.at[0])

    @pl.loop(0, 4 * ready)
    def _(h):
        copy(done.at[h], h).start()

    fill_average(average)

    @pl.loop(0, TAIL)
    def _(n):
        normalize(ready + n, late, 4 * n, mixed, q_feat, prefix, gain, total, squares, average)
        for h in range(4):
            copy(late.at[4 * n + h], 4 * (ready + n) + h).start()

    pltpu.make_async_copy(out, out, sem.at[0]).wait()


def on_device(query_seq, key_seq, value_seq, conv_kernel, feature_map, norm_gain):
    tokens, width = query_seq.shape
    dim = feature_map.shape[0]
    devices = lax.axis_size("seq")
    chunks = width // (4 * dim)
    rows = pltpu.VMEM((tokens, width), BF16)
    heads = pltpu.VMEM((width // dim, tokens, dim), BF16)
    duo = pltpu.VMEM((chunks, 2 * dim, dim), BF16)
    solo = pltpu.VMEM((chunks, dim, dim), BF16)
    dma = pltpu.SemaphoreType.DMA
    keep = pltpu.MemorySpace.VMEM
    hbm = pl.BlockSpec(memory_space=pl.ANY)
    vmem = pl.BlockSpec(memory_space=pltpu.VMEM)
    parts = pl.pallas_call(
        functools.partial(kernel, devices),
        out_shape=[
            keep((width // dim, tokens, dim), BF16),
            keep((tokens, width), F32),
            keep((width // dim, tokens, dim), BF16),
            keep((chunks, 2, 2 * dim, 2 * dim), BF16),
            keep((1, width), F32),
        ],
        in_specs=[hbm] * 6,
        out_specs=[vmem] * 5,
        scratch_shapes=[
            rows,
            rows,
            rows,
            pltpu.VMEM(conv_kernel.shape, BF16),
            pltpu.VMEM(feature_map.shape, BF16),
            pltpu.VMEM((3, RIM, width), BF16),
            pltpu.VMEM((3, HALO, width), BF16),
            pltpu.VMEM((3, HALO, width), BF16),
            pltpu.VMEM((4, 2, RIM + tokens, LANES), F32),
            pltpu.VMEM((2 * dim, 2 * dim), BF16),
            pltpu.VMEM((4, tokens, dim), BF16),
            heads,
            heads,
            pltpu.VMEM((4, tokens, tokens), BF16),
            pltpu.VMEM((2, tokens, 2 * dim), F32),
            pltpu.VMEM((2, tokens, 2 * dim), BF16),
            pltpu.VMEM((2 * dim, 2 * dim), BF16),
            pltpu.VMEM((chunks, 2 * dim, dim), F32),
            duo,
            duo,
            solo,
            solo,
            solo,
            solo,
            solo,
            solo,
            duo,
            dma((3, chunks)),
            dma((3,)),
            dma((3,)),
            dma((6,)),
            dma((3, 2)),
            dma((chunks,)),
            dma((chunks,)),
            dma((chunks,)),
            dma((chunks,)),
            dma((chunks, 2)),
        ],
        compiler_params=pltpu.CompilerParams(
            collective_id=0, has_side_effects=True, vmem_limit_bytes=40 * 1024 * 1024
        ),
        name="layer",
    )(query_seq, key_seq, value_seq, conv_kernel, feature_map, norm_gain.reshape(1, width))
    return pl.pallas_call(
        store,
        out_shape=jax.ShapeDtypeStruct((tokens, width), BF16),
        in_specs=[vmem] * 5,
        out_specs=hbm,
        scratch_shapes=[
            pltpu.VMEM((4 * TAIL, tokens, dim), BF16),
            pltpu.VMEM((2, tokens, 2 * dim), F32),
            pltpu.VMEM((2, tokens, 2 * dim), BF16),
            pltpu.VMEM((2 * dim, 2 * dim), BF16),
            dma((1,)),
        ],
        compiler_params=pltpu.CompilerParams(vmem_limit_bytes=8 * 1024 * 1024),
        name="store",
    )(*parts)


def solution(mesh):
    split = P(("groups", "seq"), None)
    return jax.shard_map(
        on_device,
        mesh=mesh,
        in_specs=(split, split, split, P(), P(), P()),
        out_specs=split,
        check_vma=False,
    )
```

```python
import functools

import jax
import jax.numpy as jnp
from jax import lax
from jax.experimental import pallas as pl
from jax.experimental.pallas import tpu as pltpu
from jax.sharding import PartitionSpec as P

MESH = pl.DeviceIdType.MESH
F32 = jnp.float32
BF16 = jnp.bfloat16
RIM = 8
HALO = 4
LANES = 128
X_LAG = 2
Y_LAG = 4
Z_LAG = 3
R_LAG = 5
P_LAG = 3
CATCH_ONE = 2
CATCH_TWO = 5
CATCH_PLANE = 3
MIX_LAG = 12
LAST_MIX_LAG = 10
TAIL = 2


def short_conv(buf, halo, taps, which, col, width, wide):
    tap_count = taps.shape[1]
    length = buf.shape[0]
    out = []
    for j in range(width // LANES):
        lanes = pl.ds(pl.multiple_of(col + j * LANES, LANES), LANES)
        tall = wide.at[j]
        tap_rows = taps[which, :, lanes].astype(F32)
        tall[RIM - HALO : RIM] = halo[which, :, lanes].astype(F32)
        parts = []
        for top in range(0, length, length // 2):
            size = length // 2
            rows = buf[top : top + size, lanes].astype(F32)
            tall[RIM + top : RIM + top + size] = rows
            total = tap_rows[0:1] * rows
            for offset in range(1, tap_count):
                start = RIM + top - offset
                total = total + tap_rows[offset : offset + 1] * tall[start : start + size]
            parts.append(total.astype(BF16))
        out.append(jnp.concatenate(parts, axis=0))
    return jnp.concatenate(out, axis=1)


def features(conv_rows, wide_map):
    projected = jnp.dot(conv_rows, wide_map[...], preferred_element_type=F32)
    return jnp.where(projected > 0, projected + 1.0, jnp.exp(projected)).astype(BF16)


def put_pair(buf, first, rows):
    dim = buf.shape[2]
    buf[first] = rows[:, :dim]
    buf[first + 1] = rows[:, dim:]


def get_pair(buf, first):
    return jnp.concatenate([buf[first], buf[first + 1]], axis=1)


def fill_average(average):
    dim = average.shape[0] // 2
    average[...] = jnp.zeros_like(average)
    average[:dim, :dim] = jnp.full((dim, dim), 1.0 / dim, BF16)
    average[dim:, dim:] = jnp.full((dim, dim), 1.0 / dim, BF16)


def normalize(c, out, first, mixed, q_feat, prefix, gain, total, squares, average):
    pair = average.shape[0]
    spans = [pl.ds(pl.multiple_of((2 * c + side) * pair, pair), pair) for side in range(2)]
    for side in range(2):
        query = get_pair(q_feat, 4 * c + 2 * side)
        rows = mixed[:, spans[side]] + jnp.dot(query, prefix[c, side], preferred_element_type=F32)
        total[side] = rows
        squares[side] = (rows * rows).astype(BF16)
    for side in range(2):
        mean = jnp.dot(squares[side], average[...], preferred_element_type=F32)
        done = (total[side] * lax.rsqrt(mean + 1e-06) * gain[:, spans[side]]).astype(BF16)
        put_pair(out, first + 2 * side, done)


def kernel(
    devices,
    q_hbm,
    k_hbm,
    v_hbm,
    taps_hbm,
    map_hbm,
    gain_hbm,
    out_buf,
    mixed,
    q_feat,
    prefix,
    gain,
    q_buf,
    k_buf,
    v_buf,
    taps,
    feature_map,
    tail,
    halo_out,
    halo,
    wide,
    wide_map,
    q_stage,
    k_feat,
    v_conv,
    weights,
    total,
    squares,
    average,
    own_state,
    x_out,
    x_in,
    raw_out,
    raw_in,
    z_out,
    z_in,
    res_out,
    res_in,
    p_out,
    load_sem,
    aux_sem,
    tail_sem,
    send_sem,
    halo_sem,
    x_sem,
    raw_sem,
    z_sem,
    res_sem,
    p_sem,
):
    tokens, width = q_buf.shape
    half = tokens // 2
    dim = feature_map.shape[0]
    pair = 2 * dim
    chunk = 2 * pair
    chunks = width // chunk
    me = lax.axis_index("seq")
    core = lax.rem(me, 2)
    y = lax.rem(me // 2, 2)
    z = me // 4
    planes = devices // 4
    partner = me + 1 - 2 * core
    across = me + 2 - 4 * y
    sources = (q_hbm, k_hbm, v_hbm)

    def load_tail(which):
        rows = pl.ds(tokens - RIM, RIM)
        return pltpu.make_async_copy(sources[which].at[rows], tail.at[which], tail_sem.at[which])

    def load(buf, which, c):
        cols = pl.ds(pl.multiple_of(c * chunk, chunk), chunk)
        return pltpu.make_async_copy(sources[which].at[:, cols], buf.at[:, cols], load_sem.at[which, c])

    small = [
        pltpu.make_async_copy(src, dst, aux_sem.at[n])
        for n, (src, dst) in enumerate(((taps_hbm, taps), (map_hbm, feature_map), (gain_hbm, gain)))
    ]
    barrier = pltpu.get_barrier_semaphore()

    def greet(target):
        pl.semaphore_signal(barrier, inc=1, device_id={"seq": target}, device_id_type=MESH)

    greet(partner)
    greet(across)

    @pl.when(me > 0)
    def _():
        greet(me - 1)

    @pl.when(me < devices - 1)
    def _():
        greet(me + 1)

    @pl.when(z > 0)
    def _():
        greet(me - 4)

    @pl.when(z < planes - 1)
    def _():
        greet(me + 4)

    load_tail(1).start()
    load_tail(2).start()
    small[0].start()
    small[1].start()

    def load_pair(c):
        load(k_buf, 1, c).start()
        load(v_buf, 2, c).start()

    load_pair(0)
    load_pair(1)

    wide_map[...] = jnp.zeros_like(wide_map)
    fill_average(average)

    @pl.when(me == 0)
    def _():
        halo[...] = jnp.zeros_like(halo)

    @pl.when(z == 0)
    def _():
        @pl.loop(0, chunks)
        def _(c):
            z_in[c] = jnp.zeros(z_in.shape[1:], BF16)

    def ready_tail(which):
        load_tail(which).wait()
        halo_out[which] = tail[which].astype(F32)[RIM - HALO :].astype(BF16)

    ready_tail(1)
    ready_tail(2)
    small[0].wait()
    small[1].wait()
    wide_map[:dim, :dim] = feature_map[...]
    wide_map[dim:, dim:] = feature_map[...]

    edges = [(me > 0), (me < devices - 1), (z > 0), (z < planes - 1)]
    pl.semaphore_wait(barrier, 2 + sum(e.astype(jnp.int32) for e in edges))

    def remote(src, dst, kind, recv_sem, target):
        return pltpu.make_async_remote_copy(
            src_ref=src,
            dst_ref=dst,
            send_sem=send_sem.at[kind],
            recv_sem=recv_sem,
            device_id={"seq": target},
            device_id_type=MESH,
        )

    def halo_copy(which, piece):
        cols = pl.ds(0, chunk) if piece == 0 else pl.ds(chunk, width - chunk)
        return remote(
            halo_out.at[which, :, cols],
            halo.at[which, :, cols],
            0,
            halo_sem.at[which, piece],
            lax.rem(me + 1, devices),
        )

    @pl.when(me < devices - 1)
    def _():
        for piece in range(2):
            for which in (1, 2):
                halo_copy(which, piece).start()

    load_tail(0).start()
    small[2].start()

    @pl.loop(2, chunks)
    def _(c):
        load_pair(c)

    @pl.loop(0, chunks)
    def _(c):
        load(q_buf, 0, c).start()

    @pl.loop(0, chunks)
    def _(c):
        blank = jnp.zeros((dim, dim), BF16)
        for side in range(2):
            prefix[c, side, :dim, dim:] = blank
            prefix[c, side, dim:, :dim] = blank

    ready_tail(0)

    @pl.when(me < devices - 1)
    def _():
        for piece in range(2):
            halo_copy(0, piece).start()

    def wait_halo(c, which):
        for piece in range(2):

            @pl.when((me > 0) & (c == piece))
            def _():
                for w in which:
                    halo_copy(w, piece).wait_recv()

    lead = pl.ds(pl.multiple_of(y * dim, dim), dim)
    other = pl.ds(pl.multiple_of((1 - y) * dim, dim), dim)

    def x_copy(c):
        return remote(x_out.at[c], x_in.at[c], 1, x_sem.at[c], partner)

    def raw_copy(c):
        return remote(raw_out.at[c], raw_in.at[c], 2, raw_sem.at[c], across)

    def z_copy(c):
        return remote(z_out.at[c], z_in.at[c], 3, z_sem.at[c], lax.rem(me + 4, devices))

    def res_copy(c):
        return remote(res_out.at[c], res_in.at[c], 4, res_sem.at[c], across)

    def p_copy(c, h):
        rows = pl.ds(pl.multiple_of(h * dim, dim), dim)
        return remote(p_out.at[c, rows], prefix.at[c, core, rows, rows], 5, p_sem.at[c, h], partner)

    def pair_state(feat, v_rows):
        both = lax.dot_general(feat, v_rows, (((0,), (0,)), ((), ())), preferred_element_type=F32)
        return both[:dim, :dim], both[dim:, dim:]

    def keep_own(c):
        first_head = 4 * c + 2 * core
        first, second = pair_state(get_pair(k_feat, first_head), get_pair(v_conv, first_head))
        own_state[c, :dim] = first
        own_state[c, dim:] = second

    def states(c):
        load(k_buf, 1, c).wait()
        load(v_buf, 2, c).wait()
        wait_halo(c, (1, 2))
        keep_own(jnp.maximum(c - 1, 0))
        turns = (1 - core, core)
        heads = [4 * c + 2 * turn for turn in turns]
        cols = [pl.multiple_of(c * chunk + turn * pair, pair) for turn in turns]

        def key_rows(side):
            return short_conv(k_buf, halo, taps, 1, cols[side], pair, wide.at[2 * side])

        def value_rows(side):
            return short_conv(v_buf, halo, taps, 2, cols[side], pair, wide.at[2 * side + 1])

        key_0 = key_rows(0)
        feat_0 = features(key_0, wide_map)
        key_1 = key_rows(1)
        put_pair(k_feat, heads[0], feat_0)
        values_0 = value_rows(0)
        put_pair(v_conv, heads[0], values_0)
        put_pair(k_feat, heads[1], features(key_1, wide_map))
        first, second = pair_state(feat_0, values_0)
        put_pair(v_conv, heads[1], value_rows(1))
        x_out[c, :dim] = first.astype(BF16)
        x_out[c, dim:] = second.astype(BF16)
        x_copy(c).start()

    def relay_raw(c):
        x_copy(c).wait_recv()
        raw_out[c] = (own_state[c, other] + x_in[c, other].astype(F32)).astype(BF16)
        raw_copy(c).start()

    def hand_on(c, h, rows, earlier):
        p_out[c, rows] = (earlier + jnp.where(core == 0, own_state[c, rows], 0.0)).astype(BF16)
        p_copy(c, h).start()
        own = earlier + jnp.where(core == 1, x_in[c, rows].astype(F32), 0.0)
        prefix[c, core, rows, rows] = own.astype(BF16)

    z_lag = X_LAG + Y_LAG + Z_LAG * z
    raw_end = chunks + X_LAG

    def relay_z(c, step):
        raw_copy(c).wait_recv()

        @pl.when(z > 0)
        def _():
            z_copy(c).wait_recv()

        before = z_in[c].astype(F32)
        chip = own_state[c, lead] + x_in[c, lead].astype(F32)
        far = raw_in[c].astype(F32)
        z_out[c] = (before + chip + far).astype(BF16)

        @pl.when(z < planes - 1)
        def _():
            z_copy(c).start()

        res_out[c] = (before + jnp.where(y == 0, chip, 0.0)).astype(BF16)

        @pl.when(step >= raw_end)
        def _():
            res_copy(c).start()

        hand_on(c, y, lead, before + jnp.where(y == 1, far, 0.0))

    def relay_res(c):
        res_copy(c).wait_recv()
        hand_on(c, 1 - y, other, res_in[c].astype(F32))

    def mix_values(c, head):
        cols = pl.ds(pl.multiple_of(c * chunk + head * dim, dim), dim)
        values = v_conv[4 * c + head]
        mixed[:half, cols] = jnp.dot(weights[head, :half, :half], values[:half], preferred_element_type=F32)
        mixed[half:, cols] = jnp.dot(weights[head, half:], values, preferred_element_type=F32)

    def query_rows(c, side):
        return short_conv(q_buf, halo, taps, 0, c * chunk + side * pair, pair, wide.at[side])

    def query_feat(c, side, rows):
        feat = features(rows, wide_map)
        put_pair(q_stage, 2 * side, feat)
        put_pair(q_feat, 4 * c + 2 * side, feat)

    def mix_scores(c, head):
        row = lax.broadcasted_iota(jnp.int32, (half, half), 0)
        causal = row >= lax.broadcasted_iota(jnp.int32, (half, half), 1)
        scores = lax.dot_general(
            q_stage[head],
            k_feat[4 * c + head],
            (((1,), (1,)), ((), ())),
            preferred_element_type=F32,
        )
        place = weights.at[head]
        place[:half, :half] = jnp.where(causal, scores[:half, :half], 0.0).astype(BF16)
        place[half:, :half] = scores[half:, :half].astype(BF16)
        place[half:, half:] = jnp.where(causal, scores[half:, half:], 0.0).astype(BF16)

    def await_query(c):
        @pl.when(c < chunks)
        def _():
            load(q_buf, 0, c).wait()
            wait_halo(c, (0,))

    def local_mix(c):
        await_query(c + 1)
        last = jnp.maximum(c - 1, 0)
        after = jnp.minimum(c + 1, chunks - 1)
        for side in range(2):
            rows = query_rows(after, side)
            mix_values(last, 2 * side)
            mix_values(last, 2 * side + 1)
            mix_scores(c, 2 * side)
            mix_scores(c, 2 * side + 1)
            query_feat(after, side, rows)

    def finish(c):
        p_copy(c, 0).wait_recv()
        p_copy(c, 1).wait_recv()

        @pl.when(c < chunks - TAIL)
        def _():
            normalize(c, out_buf, 4 * c, mixed, q_feat, prefix, gain, total, squares, average)

    mix_lag = jnp.where(z == planes - 1, LAST_MIX_LAG, MIX_LAG)
    catch = 1 + (z >= CATCH_PLANE).astype(jnp.int32)
    last_lag = jnp.maximum(jnp.maximum(raw_end, z_lag - catch) + R_LAG + P_LAG, mix_lag + 1)

    def sums_by(step):
        one = (step >= chunks + CATCH_ONE).astype(jnp.int32)
        two = ((step >= chunks + CATCH_TWO) & (z >= CATCH_PLANE)).astype(jnp.int32)
        return jnp.clip(step - z_lag + 1 + one + two, 0, chunks)

    def results_by(step):
        return jnp.minimum(sums_by(step - R_LAG), jnp.clip(step - raw_end - R_LAG + 1, 0, chunks))

    def finished_by(step):
        return jnp.minimum(results_by(step - P_LAG), jnp.clip(step - mix_lag, 0, chunks))

    def at(step, lag, work):
        c = step - lag

        @pl.when((c >= 0) & (c < chunks))
        def _():
            work(c)

    @pl.loop(0, chunks + last_lag)
    def _(step):
        at(step, 0, states)
        @pl.when(step == chunks)
        def _():
            keep_own(chunks - 1)

        at(step, X_LAG, relay_raw)

        @pl.when(step == raw_end)
        def _():
            @pl.loop(0, sums_by(step - 1))
            def _(c):
                res_copy(c).start()

        @pl.loop(sums_by(step - 1), sums_by(step))
        def _(c):
            relay_z(c, step)

        at(step, jnp.maximum(raw_end, z_lag - catch) + R_LAG, relay_res)
        @pl.when(step == mix_lag - 1)
        def _():
            small[2].wait()
            await_query(0)
            for side in range(2):
                query_feat(0, side, query_rows(0, side))

        at(step, mix_lag, local_mix)

        @pl.when(step == mix_lag + chunks)
        def _():
            for head in range(4):
                mix_values(chunks - 1, head)

        at(step, last_lag, finish)

    @pl.when(me < devices - 1)
    def _():
        remote(halo_out, halo, 0, halo_sem.at[0, 0], partner).wait_send()

    remote(x_out, x_in, 1, x_sem.at[0], partner).wait_send()
    remote(raw_out, raw_in, 2, raw_sem.at[0], across).wait_send()

    @pl.when(z < planes - 1)
    def _():
        remote(z_out, z_in, 3, z_sem.at[0], partner).wait_send()

    remote(res_out, res_in, 4, res_sem.at[0], across).wait_send()
    remote(p_out, p_out, 5, p_sem.at[0, 0], partner).wait_send()


def store(done, mixed, q_feat, prefix, gain, out, late, total, squares, average, sem):
    heads, _, dim = done.shape
    chunks = heads // 4
    ready = chunks - TAIL

    def copy(src, h):
        cols = pl.ds(pl.multiple_of(h * dim, dim), dim)
        return pltpu.make_async_copy(src, out.at[:, cols], sem.at[0])

    @pl.loop(0, 4 * ready)
    def _(h):
        copy(done.at[h], h).start()

    fill_average(average)

    @pl.loop(0, TAIL)
    def _(n):
        normalize(ready + n, late, 4 * n, mixed, q_feat, prefix, gain, total, squares, average)
        for h in range(4):
            copy(late.at[4 * n + h], 4 * (ready + n) + h).start()

    pltpu.make_async_copy(out, out, sem.at[0]).wait()


def on_device(query_seq, key_seq, value_seq, conv_kernel, feature_map, norm_gain):
    tokens, width = query_seq.shape
    dim = feature_map.shape[0]
    devices = lax.axis_size("seq")
    chunks = width // (4 * dim)
    rows = pltpu.VMEM((tokens, width), BF16)
    heads = pltpu.VMEM((width // dim, tokens, dim), BF16)
    duo = pltpu.VMEM((chunks, 2 * dim, dim), BF16)
    solo = pltpu.VMEM((chunks, dim, dim), BF16)
    dma = pltpu.SemaphoreType.DMA
    keep = pltpu.MemorySpace.VMEM
    hbm = pl.BlockSpec(memory_space=pl.ANY)
    vmem = pl.BlockSpec(memory_space=pltpu.VMEM)
    parts = pl.pallas_call(
        functools.partial(kernel, devices),
        out_shape=[
            keep((width // dim, tokens, dim), BF16),
            keep((tokens, width), F32),
            keep((width // dim, tokens, dim), BF16),
            keep((chunks, 2, 2 * dim, 2 * dim), BF16),
            keep((1, width), F32),
        ],
        in_specs=[hbm] * 6,
        out_specs=[vmem] * 5,
        scratch_shapes=[
            rows,
            rows,
            rows,
            pltpu.VMEM(conv_kernel.shape, BF16),
            pltpu.VMEM(feature_map.shape, BF16),
            pltpu.VMEM((3, RIM, width), BF16),
            pltpu.VMEM((3, HALO, width), BF16),
            pltpu.VMEM((3, HALO, width), BF16),
            pltpu.VMEM((4, 2, RIM + tokens, LANES), F32),
            pltpu.VMEM((2 * dim, 2 * dim), BF16),
            pltpu.VMEM((4, tokens, dim), BF16),
            heads,
            heads,
            pltpu.VMEM((4, tokens, tokens), BF16),
            pltpu.VMEM((2, tokens, 2 * dim), F32),
            pltpu.VMEM((2, tokens, 2 * dim), BF16),
            pltpu.VMEM((2 * dim, 2 * dim), BF16),
            pltpu.VMEM((chunks, 2 * dim, dim), F32),
            duo,
            duo,
            solo,
            solo,
            solo,
            solo,
            solo,
            solo,
            duo,
            dma((3, chunks)),
            dma((3,)),
            dma((3,)),
            dma((6,)),
            dma((3, 2)),
            dma((chunks,)),
            dma((chunks,)),
            dma((chunks,)),
            dma((chunks,)),
            dma((chunks, 2)),
        ],
        compiler_params=pltpu.CompilerParams(
            collective_id=0, has_side_effects=True, vmem_limit_bytes=40 * 1024 * 1024
        ),
        name="layer",
    )(query_seq, key_seq, value_seq, conv_kernel, feature_map, norm_gain.reshape(1, width))
    return pl.pallas_call(
        store,
        out_shape=jax.ShapeDtypeStruct((tokens, width), BF16),
        in_specs=[vmem] * 5,
        out_specs=hbm,
        scratch_shapes=[
            pltpu.VMEM((4 * TAIL, tokens, dim), BF16),
            pltpu.VMEM((2, tokens, 2 * dim), F32),
            pltpu.VMEM((2, tokens, 2 * dim), BF16),
            pltpu.VMEM((2 * dim, 2 * dim), BF16),
            dma((1,)),
        ],
        compiler_params=pltpu.CompilerParams(vmem_limit_bytes=8 * 1024 * 1024),
        name="store",
    )(*parts)


def solution(mesh):
    split = P(("groups", "seq"), None)
    return jax.shard_map(
        on_device,
        mesh=mesh,
        in_specs=(split, split, split, P(), P(), P()),
        out_specs=split,
        check_vma=False,
    )
```

```python
import functools

import jax
import jax.numpy as jnp
from jax import lax
from jax.experimental import pallas as pl
from jax.experimental.pallas import tpu as pltpu
from jax.sharding import PartitionSpec as P

MESH = pl.DeviceIdType.MESH
F32 = jnp.float32
BF16 = jnp.bfloat16
RIM = 8
HALO = 4
LANES = 128
X_LAG = 2
Y_LAG = 4
Z_LAG = 3
R_LAG = 5
P_LAG = 3
CATCH_ONE = 3
CATCH_TWO = 6
CATCH_PLANE = 3
MIX_LAG = 12
LAST_MIX_LAG = 10
TAIL = 2


def short_conv(buf, halo, taps, which, col, width, wide):
    tap_count = taps.shape[1]
    length = buf.shape[0]
    out = []
    for j in range(width // LANES):
        lanes = pl.ds(pl.multiple_of(col + j * LANES, LANES), LANES)
        tall = wide.at[j]
        tap_rows = taps[which, :, lanes].astype(F32)
        tall[RIM - HALO : RIM] = halo[which, :, lanes].astype(F32)
        parts = []
        for top in range(0, length, length // 2):
            size = length // 2
            rows = buf[top : top + size, lanes].astype(F32)
            tall[RIM + top : RIM + top + size] = rows
            total = tap_rows[0:1] * rows
            for offset in range(1, tap_count):
                start = RIM + top - offset
                total = total + tap_rows[offset : offset + 1] * tall[start : start + size]
            parts.append(total.astype(BF16))
        out.append(jnp.concatenate(parts, axis=0))
    return jnp.concatenate(out, axis=1)


def features(conv_rows, wide_map):
    projected = jnp.dot(conv_rows, wide_map[...], preferred_element_type=F32)
    return jnp.where(projected > 0, projected + 1.0, jnp.exp(projected)).astype(BF16)


def put_pair(buf, first, rows):
    dim = buf.shape[2]
    buf[first] = rows[:, :dim]
    buf[first + 1] = rows[:, dim:]


def get_pair(buf, first):
    return jnp.concatenate([buf[first], buf[first + 1]], axis=1)


def fill_average(average):
    dim = average.shape[0] // 2
    average[...] = jnp.zeros_like(average)
    average[:dim, :dim] = jnp.full((dim, dim), 1.0 / dim, BF16)
    average[dim:, dim:] = jnp.full((dim, dim), 1.0 / dim, BF16)


def normalize(c, out, first, mixed, q_feat, prefix, gain, total, squares, average):
    pair = average.shape[0]
    spans = [pl.ds(pl.multiple_of((2 * c + side) * pair, pair), pair) for side in range(2)]
    for side in range(2):
        query = get_pair(q_feat, 4 * c + 2 * side)
        rows = mixed[:, spans[side]] + jnp.dot(query, prefix[c, side], preferred_element_type=F32)
        total[side] = rows
        squares[side] = (rows * rows).astype(BF16)
    for side in range(2):
        mean = jnp.dot(squares[side], average[...], preferred_element_type=F32)
        done = (total[side] * lax.rsqrt(mean + 1e-06) * gain[:, spans[side]]).astype(BF16)
        put_pair(out, first + 2 * side, done)


def kernel(
    devices,
    q_hbm,
    k_hbm,
    v_hbm,
    taps_hbm,
    map_hbm,
    gain_hbm,
    out_buf,
    mixed,
    q_feat,
    prefix,
    gain,
    q_buf,
    k_buf,
    v_buf,
    taps,
    feature_map,
    tail,
    halo_out,
    halo,
    wide,
    wide_map,
    q_stage,
    k_feat,
    v_conv,
    weights,
    total,
    squares,
    average,
    own_state,
    x_out,
    x_in,
    raw_out,
    raw_in,
    z_out,
    z_in,
    res_out,
    res_in,
    p_out,
    load_sem,
    aux_sem,
    tail_sem,
    send_sem,
    halo_sem,
    x_sem,
    raw_sem,
    z_sem,
    res_sem,
    p_sem,
):
    tokens, width = q_buf.shape
    half = tokens // 2
    dim = feature_map.shape[0]
    pair = 2 * dim
    chunk = 2 * pair
    chunks = width // chunk
    me = lax.axis_index("seq")
    core = lax.rem(me, 2)
    y = lax.rem(me // 2, 2)
    z = me // 4
    planes = devices // 4
    partner = me + 1 - 2 * core
    across = me + 2 - 4 * y
    sources = (q_hbm, k_hbm, v_hbm)

    def load_tail(which):
        rows = pl.ds(tokens - RIM, RIM)
        return pltpu.make_async_copy(sources[which].at[rows], tail.at[which], tail_sem.at[which])

    def load(buf, which, c):
        cols = pl.ds(pl.multiple_of(c * chunk, chunk), chunk)
        return pltpu.make_async_copy(sources[which].at[:, cols], buf.at[:, cols], load_sem.at[which, c])

    small = [
        pltpu.make_async_copy(src, dst, aux_sem.at[n])
        for n, (src, dst) in enumerate(((taps_hbm, taps), (map_hbm, feature_map), (gain_hbm, gain)))
    ]
    barrier = pltpu.get_barrier_semaphore()

    def greet(target):
        pl.semaphore_signal(barrier, inc=1, device_id={"seq": target}, device_id_type=MESH)

    greet(partner)
    greet(across)

    @pl.when(me > 0)
    def _():
        greet(me - 1)

    @pl.when(me < devices - 1)
    def _():
        greet(me + 1)

    @pl.when(z > 0)
    def _():
        greet(me - 4)

    @pl.when(z < planes - 1)
    def _():
        greet(me + 4)

    load_tail(1).start()
    load_tail(2).start()
    small[0].start()
    small[1].start()

    def load_pair(c):
        load(k_buf, 1, c).start()
        load(v_buf, 2, c).start()

    load_pair(0)
    load_pair(1)

    wide_map[...] = jnp.zeros_like(wide_map)
    fill_average(average)

    @pl.when(me == 0)
    def _():
        halo[...] = jnp.zeros_like(halo)

    @pl.when(z == 0)
    def _():
        @pl.loop(0, chunks)
        def _(c):
            z_in[c] = jnp.zeros(z_in.shape[1:], BF16)

    def ready_tail(which):
        load_tail(which).wait()
        halo_out[which] = tail[which].astype(F32)[RIM - HALO :].astype(BF16)

    ready_tail(1)
    ready_tail(2)
    small[0].wait()
    small[1].wait()
    wide_map[:dim, :dim] = feature_map[...]
    wide_map[dim:, dim:] = feature_map[...]

    edges = [(me > 0), (me < devices - 1), (z > 0), (z < planes - 1)]
    pl.semaphore_wait(barrier, 2 + sum(e.astype(jnp.int32) for e in edges))

    def remote(src, dst, kind, recv_sem, target):
        return pltpu.make_async_remote_copy(
            src_ref=src,
            dst_ref=dst,
            send_sem=send_sem.at[kind],
            recv_sem=recv_sem,
            device_id={"seq": target},
            device_id_type=MESH,
        )

    def halo_copy(which, piece):
        cols = pl.ds(0, chunk) if piece == 0 else pl.ds(chunk, width - chunk)
        return remote(
            halo_out.at[which, :, cols],
            halo.at[which, :, cols],
            0,
            halo_sem.at[which, piece],
            lax.rem(me + 1, devices),
        )

    @pl.when(me < devices - 1)
    def _():
        for piece in range(2):
            for which in (1, 2):
                halo_copy(which, piece).start()

    load_tail(0).start()
    small[2].start()

    @pl.loop(2, chunks)
    def _(c):
        load_pair(c)

    @pl.loop(0, chunks)
    def _(c):
        load(q_buf, 0, c).start()

    @pl.loop(0, chunks)
    def _(c):
        blank = jnp.zeros((dim, dim), BF16)
        for side in range(2):
            prefix[c, side, :dim, dim:] = blank
            prefix[c, side, dim:, :dim] = blank

    ready_tail(0)

    @pl.when(me < devices - 1)
    def _():
        for piece in range(2):
            halo_copy(0, piece).start()

    def wait_halo(c, which):
        for piece in range(2):

            @pl.when((me > 0) & (c == piece))
            def _():
                for w in which:
                    halo_copy(w, piece).wait_recv()

    lead = pl.ds(pl.multiple_of(y * dim, dim), dim)
    other = pl.ds(pl.multiple_of((1 - y) * dim, dim), dim)

    def x_copy(c):
        return remote(x_out.at[c], x_in.at[c], 1, x_sem.at[c], partner)

    def raw_copy(c):
        return remote(raw_out.at[c], raw_in.at[c], 2, raw_sem.at[c], across)

    def z_copy(c):
        return remote(z_out.at[c], z_in.at[c], 3, z_sem.at[c], lax.rem(me + 4, devices))

    def res_copy(c):
        return remote(res_out.at[c], res_in.at[c], 4, res_sem.at[c], across)

    def p_copy(c, h):
        rows = pl.ds(pl.multiple_of(h * dim, dim), dim)
        return remote(p_out.at[c, rows], prefix.at[c, core, rows, rows], 5, p_sem.at[c, h], partner)

    def pair_state(feat, v_rows):
        both = lax.dot_general(feat, v_rows, (((0,), (0,)), ((), ())), preferred_element_type=F32)
        return both[:dim, :dim], both[dim:, dim:]

    def keep_own(c):
        first_head = 4 * c + 2 * core
        first, second = pair_state(get_pair(k_feat, first_head), get_pair(v_conv, first_head))
        own_state[c, :dim] = first
        own_state[c, dim:] = second

    def states(c):
        load(k_buf, 1, c).wait()
        load(v_buf, 2, c).wait()
        wait_halo(c, (1, 2))
        keep_own(jnp.maximum(c - 1, 0))
        turns = (1 - core, core)
        heads = [4 * c + 2 * turn for turn in turns]
        cols = [pl.multiple_of(c * chunk + turn * pair, pair) for turn in turns]

        def key_rows(side):
            return short_conv(k_buf, halo, taps, 1, cols[side], pair, wide.at[2 * side])

        def value_rows(side):
            return short_conv(v_buf, halo, taps, 2, cols[side], pair, wide.at[2 * side + 1])

        key_0 = key_rows(0)
        feat_0 = features(key_0, wide_map)
        key_1 = key_rows(1)
        put_pair(k_feat, heads[0], feat_0)
        values_0 = value_rows(0)
        put_pair(v_conv, heads[0], values_0)
        put_pair(k_feat, heads[1], features(key_1, wide_map))
        first, second = pair_state(feat_0, values_0)
        put_pair(v_conv, heads[1], value_rows(1))
        x_out[c, :dim] = first.astype(BF16)
        x_out[c, dim:] = second.astype(BF16)
        x_copy(c).start()

    def relay_raw(c):
        x_copy(c).wait_recv()
        raw_out[c] = (own_state[c, other] + x_in[c, other].astype(F32)).astype(BF16)
        raw_copy(c).start()

    def hand_on(c, h, rows, earlier):
        p_out[c, rows] = (earlier + jnp.where(core == 0, own_state[c, rows], 0.0)).astype(BF16)
        p_copy(c, h).start()
        own = earlier + jnp.where(core == 1, x_in[c, rows].astype(F32), 0.0)
        prefix[c, core, rows, rows] = own.astype(BF16)

    z_lag = X_LAG + Y_LAG + Z_LAG * z
    raw_end = chunks + X_LAG

    def relay_z(c, step):
        raw_copy(c).wait_recv()

        @pl.when(z > 0)
        def _():
            z_copy(c).wait_recv()

        before = z_in[c].astype(F32)
        chip = own_state[c, lead] + x_in[c, lead].astype(F32)
        far = raw_in[c].astype(F32)
        z_out[c] = (before + chip + far).astype(BF16)

        @pl.when(z < planes - 1)
        def _():
            z_copy(c).start()

        res_out[c] = (before + jnp.where(y == 0, chip, 0.0)).astype(BF16)

        @pl.when(step >= raw_end)
        def _():
            res_copy(c).start()

        hand_on(c, y, lead, before + jnp.where(y == 1, far, 0.0))

    def relay_res(c):
        res_copy(c).wait_recv()
        hand_on(c, 1 - y, other, res_in[c].astype(F32))

    def mix_values(c, head):
        cols = pl.ds(pl.multiple_of(c * chunk + head * dim, dim), dim)
        values = v_conv[4 * c + head]
        mixed[:half, cols] = jnp.dot(weights[head, :half, :half], values[:half], preferred_element_type=F32)
        mixed[half:, cols] = jnp.dot(weights[head, half:], values, preferred_element_type=F32)

    def query_rows(c, side):
        return short_conv(q_buf, halo, taps, 0, c * chunk + side * pair, pair, wide.at[side])

    def query_feat(c, side, rows):
        feat = features(rows, wide_map)
        put_pair(q_stage, 2 * side, feat)
        put_pair(q_feat, 4 * c + 2 * side, feat)

    def mix_scores(c, head):
        row = lax.broadcasted_iota(jnp.int32, (half, half), 0)
        causal = row >= lax.broadcasted_iota(jnp.int32, (half, half), 1)
        scores = lax.dot_general(
            q_stage[head],
            k_feat[4 * c + head],
            (((1,), (1,)), ((), ())),
            preferred_element_type=F32,
        )
        place = weights.at[head]
        place[:half, :half] = jnp.where(causal, scores[:half, :half], 0.0).astype(BF16)
        place[half:, :half] = scores[half:, :half].astype(BF16)
        place[half:, half:] = jnp.where(causal, scores[half:, half:], 0.0).astype(BF16)

    def await_query(c):
        @pl.when(c < chunks)
        def _():
            load(q_buf, 0, c).wait()
            wait_halo(c, (0,))

    def local_mix(c):
        await_query(c + 1)
        last = jnp.maximum(c - 1, 0)
        after = jnp.minimum(c + 1, chunks - 1)
        for side in range(2):
            rows = query_rows(after, side)
            mix_values(last, 2 * side)
            mix_values(last, 2 * side + 1)
            mix_scores(c, 2 * side)
            mix_scores(c, 2 * side + 1)
            query_feat(after, side, rows)

    def finish(c):
        p_copy(c, 0).wait_recv()
        p_copy(c, 1).wait_recv()

        @pl.when(c < chunks - TAIL)
        def _():
            normalize(c, out_buf, 4 * c, mixed, q_feat, prefix, gain, total, squares, average)

    mix_lag = jnp.where(z == planes - 1, LAST_MIX_LAG, MIX_LAG)
    catch = 1 + (z >= CATCH_PLANE).astype(jnp.int32)
    last_lag = jnp.maximum(jnp.maximum(raw_end, z_lag - catch) + R_LAG + P_LAG, mix_lag + 1)

    def sums_by(step):
        one = (step >= chunks + CATCH_ONE).astype(jnp.int32)
        two = ((step >= chunks + CATCH_TWO) & (z >= CATCH_PLANE)).astype(jnp.int32)
        return jnp.clip(step - z_lag + 1 + one + two, 0, chunks)

    def results_by(step):
        return jnp.minimum(sums_by(step - R_LAG), jnp.clip(step - raw_end - R_LAG + 1, 0, chunks))

    def finished_by(step):
        return jnp.minimum(results_by(step - P_LAG), jnp.clip(step - mix_lag, 0, chunks))

    def at(step, lag, work):
        c = step - lag

        @pl.when((c >= 0) & (c < chunks))
        def _():
            work(c)

    @pl.loop(0, chunks + last_lag)
    def _(step):
        at(step, 0, states)
        @pl.when(step == chunks)
        def _():
            keep_own(chunks - 1)

        at(step, X_LAG, relay_raw)

        @pl.when(step == raw_end)
        def _():
            @pl.loop(0, sums_by(step - 1))
            def _(c):
                res_copy(c).start()

        @pl.loop(sums_by(step - 1), sums_by(step))
        def _(c):
            relay_z(c, step)

        at(step, jnp.maximum(raw_end, z_lag - catch) + R_LAG, relay_res)
        @pl.when(step == mix_lag - 1)
        def _():
            small[2].wait()
            await_query(0)
            for side in range(2):
                query_feat(0, side, query_rows(0, side))

        at(step, mix_lag, local_mix)

        @pl.when(step == mix_lag + chunks)
        def _():
            for head in range(4):
                mix_values(chunks - 1, head)

        at(step, last_lag, finish)

    @pl.when(me < devices - 1)
    def _():
        remote(halo_out, halo, 0, halo_sem.at[0, 0], partner).wait_send()

    remote(x_out, x_in, 1, x_sem.at[0], partner).wait_send()
    remote(raw_out, raw_in, 2, raw_sem.at[0], across).wait_send()

    @pl.when(z < planes - 1)
    def _():
        remote(z_out, z_in, 3, z_sem.at[0], partner).wait_send()

    remote(res_out, res_in, 4, res_sem.at[0], across).wait_send()
    remote(p_out, p_out, 5, p_sem.at[0, 0], partner).wait_send()


def store(done, mixed, q_feat, prefix, gain, out, late, total, squares, average, sem):
    heads, _, dim = done.shape
    chunks = heads // 4
    ready = chunks - TAIL

    def copy(src, h):
        cols = pl.ds(pl.multiple_of(h * dim, dim), dim)
        return pltpu.make_async_copy(src, out.at[:, cols], sem.at[0])

    @pl.loop(0, 4 * ready)
    def _(h):
        copy(done.at[h], h).start()

    fill_average(average)

    @pl.loop(0, TAIL)
    def _(n):
        normalize(ready + n, late, 4 * n, mixed, q_feat, prefix, gain, total, squares, average)
        for h in range(4):
            copy(late.at[4 * n + h], 4 * (ready + n) + h).start()

    pltpu.make_async_copy(out, out, sem.at[0]).wait()


def on_device(query_seq, key_seq, value_seq, conv_kernel, feature_map, norm_gain):
    tokens, width = query_seq.shape
    dim = feature_map.shape[0]
    devices = lax.axis_size("seq")
    chunks = width // (4 * dim)
    rows = pltpu.VMEM((tokens, width), BF16)
    heads = pltpu.VMEM((width // dim, tokens, dim), BF16)
    duo = pltpu.VMEM((chunks, 2 * dim, dim), BF16)
    solo = pltpu.VMEM((chunks, dim, dim), BF16)
    dma = pltpu.SemaphoreType.DMA
    keep = pltpu.MemorySpace.VMEM
    hbm = pl.BlockSpec(memory_space=pl.ANY)
    vmem = pl.BlockSpec(memory_space=pltpu.VMEM)
    parts = pl.pallas_call(
        functools.partial(kernel, devices),
        out_shape=[
            keep((width // dim, tokens, dim), BF16),
            keep((tokens, width), F32),
            keep((width // dim, tokens, dim), BF16),
            keep((chunks, 2, 2 * dim, 2 * dim), BF16),
            keep((1, width), F32),
        ],
        in_specs=[hbm] * 6,
        out_specs=[vmem] * 5,
        scratch_shapes=[
            rows,
            rows,
            rows,
            pltpu.VMEM(conv_kernel.shape, BF16),
            pltpu.VMEM(feature_map.shape, BF16),
            pltpu.VMEM((3, RIM, width), BF16),
            pltpu.VMEM((3, HALO, width), BF16),
            pltpu.VMEM((3, HALO, width), BF16),
            pltpu.VMEM((4, 2, RIM + tokens, LANES), F32),
            pltpu.VMEM((2 * dim, 2 * dim), BF16),
            pltpu.VMEM((4, tokens, dim), BF16),
            heads,
            heads,
            pltpu.VMEM((4, tokens, tokens), BF16),
            pltpu.VMEM((2, tokens, 2 * dim), F32),
            pltpu.VMEM((2, tokens, 2 * dim), BF16),
            pltpu.VMEM((2 * dim, 2 * dim), BF16),
            pltpu.VMEM((chunks, 2 * dim, dim), F32),
            duo,
            duo,
            solo,
            solo,
            solo,
            solo,
            solo,
            solo,
            duo,
            dma((3, chunks)),
            dma((3,)),
            dma((3,)),
            dma((6,)),
            dma((3, 2)),
            dma((chunks,)),
            dma((chunks,)),
            dma((chunks,)),
            dma((chunks,)),
            dma((chunks, 2)),
        ],
        compiler_params=pltpu.CompilerParams(
            collective_id=0, has_side_effects=True, vmem_limit_bytes=40 * 1024 * 1024
        ),
        name="layer",
    )(query_seq, key_seq, value_seq, conv_kernel, feature_map, norm_gain.reshape(1, width))
    return pl.pallas_call(
        store,
        out_shape=jax.ShapeDtypeStruct((tokens, width), BF16),
        in_specs=[vmem] * 5,
        out_specs=hbm,
        scratch_shapes=[
            pltpu.VMEM((4 * TAIL, tokens, dim), BF16),
            pltpu.VMEM((2, tokens, 2 * dim), F32),
            pltpu.VMEM((2, tokens, 2 * dim), BF16),
            pltpu.VMEM((2 * dim, 2 * dim), BF16),
            dma((1,)),
        ],
        compiler_params=pltpu.CompilerParams(vmem_limit_bytes=8 * 1024 * 1024),
        name="store",
    )(*parts)


def solution(mesh):
    split = P(("groups", "seq"), None)
    return jax.shard_map(
        on_device,
        mesh=mesh,
        in_specs=(split, split, split, P(), P(), P()),
        out_specs=split,
        check_vma=False,
    )
```
